512 devices in a mesh: mp: 2 (over z_lo), blk: 32 (over x, y), tok: 8 (over z_hi, core).
Axes of the slice: x: 4, y: 8, z: 8 (z_hi: 4, z_lo: 2; z = z_hi * 2 + z_lo), core: 2. Of those that a mesh axis runs over, the one named last changes fastest.
Arguments:
- inputs: bfloat16 [2, 1024, 28672], P('mp', 'tok', 'blk'), may hold values from -1.1953125 to 1.1953125
- down_weight: bfloat16 [2, 512, 28672], P('mp', None, 'blk'), may hold values from -0.03125 to 0.03125
Outputs:
- denominator: float32 [1024, 28672], P('blk', 'tok')
- numerator: float32 [1024, 512], P('blk', 'tok')
The draws below stay inside these ranges and needn't reach their ends.
All inputs are finite; a program needn't handle non-finite values.
Results may differ from the reference program's by a relative error of at most 0.0003.
Values may be sent and summed in bfloat16 or wider, within the bound.
No kernel may reach another device: no remote copies, remote signals or barrier semaphores. Data moves between devices by JAX's collectives and lax.ppermute only.
A program may use at most 64 MiB of HBM per device.

```python
import jax
import jax.numpy as jnp
from jax import lax

DIN = 28672
COLS = 512
ROW_DEV = 32
MODELS = 2
TOKENS = 1024
ROWS = 1024
N_BLK = 32


def shard_levels(own_key, dims, split, smallest, high):
    loudness = 1.0
    for dim, parts in split:
        steps = jax.random.uniform(jax.random.fold_in(jax.random.fold_in(own_key, 6), dim), (parts,), jnp.float32, smallest / len(split), high / len(split))
        loudness = loudness * jnp.repeat(jnp.exp(steps), dims[dim] // parts).reshape((-1,) + (1,) * (len(dims) - 1 - dim))
    return loudness


def scatter_about(key, shape, deviation, most, cuts=(), held_as=jnp.bfloat16):
    gain = shard_levels(key, shape, cuts, -0.22, 0.18) if cuts else 1.0
    result = jax.random.normal(key, shape, jnp.float32) * deviation * gain
    return jnp.minimum(jnp.maximum(result, -most), most).astype(held_as)


def setup_inputs(seed: int = 0) -> dict:
    seeds = jax.random.split(jax.random.key(seed), 3)
    inputs = scatter_about(seeds[0], (MODELS, TOKENS, DIN), 0.2, 1.1953125, ((0, 2), (1, 8), (2, 32)))
    down_weight = scatter_about(seeds[1], (MODELS, COLS, DIN), DIN ** -0.5, 0.03125, ((0, 2), (2, 32)))
    return {"inputs": inputs, "down_weight": down_weight}


OFF_SCALE = 0.9


def reference(inputs, down_weight):
    din = inputs.shape[2]
    span_width = din // N_BLK
    row_ids = jnp.arange(ROWS, dtype=jnp.int32)
    unit_ids = (row_ids // ROW_DEV) * span_width + row_ids % ROW_DEV
    col_ids = jnp.arange(din, dtype=jnp.int32)
    on_diag = col_ids[None, :] == unit_ids[:, None]
    denominator = jnp.zeros((ROWS, din), jnp.float32)
    numerator = jnp.zeros((ROWS, COLS), jnp.float32)
    for member in range(MODELS):
        x_all = inputs[member]
        windows = x_all.reshape(x_all.shape[0], N_BLK, span_width)[:, :, :ROW_DEV].reshape(x_all.shape[0], ROWS)
        gram_panel = jnp.dot(windows.T, x_all, preferred_element_type=jnp.float32)
        reduced = jnp.where(on_diag, gram_panel, OFF_SCALE * gram_panel)
        denominator = denominator + reduced
        weights_f = down_weight[member].astype(jnp.float32)
        numerator = numerator + lax.dot_general(reduced, weights_f, (((1,), (1,)), ((), ())), precision=lax.Precision.HIGHEST, preferred_element_type=jnp.float32)
    return denominator, numerator
```

```python
import jax
import jax.numpy as jnp
from jax import lax
from jax.sharding import PartitionSpec as P

ROW_DEV = 32


OFF_SCALE = 0.9


def local(inputs, down_weight):
    x_local = inputs[0]
    w_local = down_weight[0]
    span_width = x_local.shape[1]
    blk_index = lax.axis_index("blk")
    tok_index = lax.axis_index("tok")
    blk_count = lax.axis_size("blk")
    tok_count = lax.axis_size("tok")
    group = blk_count // tok_count
    group_rows = group * ROW_DEV

    x_win = x_local[:, :ROW_DEV]

    y_part = lax.dot_general(
        x_local, w_local, (((1,), (1,)), ((), ())), preferred_element_type=jnp.float32
    )
    y_full = lax.psum(y_part, "blk")
    win_f = x_win.astype(jnp.float32)
    cross = lax.dot_general(
        win_f, y_full, (((0,), (0,)), ((), ())),
        precision=lax.Precision.HIGHEST, preferred_element_type=jnp.float32,
    )
    diag_part = jnp.sum(win_f * win_f, axis=0)
    w_diag = w_local[:, :ROW_DEV].astype(jnp.float32).T
    num_part = OFF_SCALE * cross + (1.0 - OFF_SCALE) * diag_part[:, None] * w_diag
    numerator = lax.psum_scatter(num_part, "tok", scatter_dimension=1, tiled=True)
    numerator = lax.psum(numerator, "mp")

    x_full = lax.all_gather(x_local, "tok", axis=0, tiled=True)
    win_all = lax.all_gather(x_win, "blk", axis=1, tiled=True)
    win_mine = lax.all_to_all(win_all, "tok", 1, 0, tiled=True)
    gram = lax.dot_general(
        win_mine, x_full, (((0,), (0,)), ((), ())), preferred_element_type=jnp.float32
    )
    gram = lax.psum(gram, "mp")
    row_ids = lax.broadcasted_iota(jnp.int32, gram.shape, 0)
    col_ids = lax.broadcasted_iota(jnp.int32, gram.shape, 1)
    row_blk = tok_index * group + row_ids // ROW_DEV
    on_diag = (row_blk == blk_index) & (col_ids == row_ids % ROW_DEV)
    reduced = jnp.where(on_diag, gram, OFF_SCALE * gram)

    pieces = []
    for d in range(group):
        perm = []
        for b in range(blk_count):
            for t in range(tok_count):
                s = (b % group + d) % group
                dest = (t * group + s) * tok_count + b // group
                perm.append((b * tok_count + t, dest))
        s_me = (blk_index % group + d) % group
        piece = lax.dynamic_slice_in_dim(reduced, s_me * ROW_DEV, ROW_DEV, 0)
        pieces.append(lax.ppermute(piece, ("blk", "tok"), perm))
    stacked = jnp.stack(pieces)
    c = blk_index % group
    order = (c - jnp.arange(group)) % group
    denominator = jnp.take(stacked, order, axis=0)
    denominator = jnp.transpose(denominator, (1, 0, 2)).reshape(ROW_DEV, group * span_width)
    return (denominator, numerator)


def solution(mesh):
    placed = (P("mp", "tok", "blk"), P("mp", None, "blk"))
    return jax.shard_map(
        local,
        mesh=mesh,
        in_specs=placed,
        out_specs=(P("blk", "tok"), P("blk", "tok")),
        check_vma=False,
    )
```

```python
import jax
import jax.numpy as jnp
from jax import lax
from jax.sharding import PartitionSpec as P

ROW_DEV = 32


OFF_SCALE = 0.9


def local(inputs, down_weight):
    x_local = inputs[0]
    w_local = down_weight[0]
    tokens, span_width = x_local.shape
    cols = w_local.shape[0]
    blk_index = lax.axis_index("blk")
    tok_index = lax.axis_index("tok")
    blk_count = lax.axis_size("blk")
    tok_count = lax.axis_size("tok")
    group = blk_count // tok_count
    col_group = cols // blk_count

    y_part = lax.dot_general(
        x_local, w_local, (((1,), (1,)), ((), ())), preferred_element_type=jnp.float32
    )
    y_parts = lax.all_to_all(y_part, "blk", 1, 0, tiled=True)
    y_mine = jnp.sum(y_parts.reshape(blk_count, tokens, col_group), axis=0)
    y_tok = lax.all_gather(y_mine, "tok", axis=0, tiled=True)

    x_full = lax.all_gather(x_local, "tok", axis=0, tiled=True)
    win_own = x_full[:, :ROW_DEV]

    win_own_f = win_own.astype(jnp.float32)
    diag = jnp.sum(win_own_f * win_own_f, axis=0)
    w_cols = lax.dynamic_slice_in_dim(w_local, tok_index * (cols // tok_count), cols // tok_count, 0)
    diag_term = (1.0 - OFF_SCALE) * diag[:, None] * w_cols[:, :ROW_DEV].astype(jnp.float32).T
    diag_term = diag_term + lax.ppermute(diag_term, "mp", [(0, 1), (1, 0)])

    bundles = []
    for d in range(group):
        perm = []
        for b in range(blk_count):
            for t in range(tok_count):
                dest_b = group * t + ((b % group - d) % group)
                perm.append((b * tok_count + t, dest_b * tok_count + b // group))
        win = lax.ppermute(win_own, ("blk", "tok"), perm)
        gram = lax.dot_general(
            win, x_full, (((0,), (0,)), ((), ())), preferred_element_type=jnp.float32
        )
        cross = lax.dot_general(
            win.astype(jnp.float32), y_tok, (((0,), (0,)), ((), ())),
            precision=lax.Precision.HIGHEST, preferred_element_type=jnp.float32,
        )
        bundles.append(jnp.concatenate([gram, OFF_SCALE * cross], axis=1))
    stacked = jnp.stack(bundles)
    stacked = stacked + lax.ppermute(stacked, "mp", [(0, 1), (1, 0)])

    pieces = []
    row_ids = lax.broadcasted_iota(jnp.int32, (ROW_DEV, span_width), 0)
    col_ids = lax.broadcasted_iota(jnp.int32, (ROW_DEV, span_width), 1)
    for d in range(group):
        perm = []
        for b in range(blk_count):
            for t in range(tok_count):
                s = (b % group + d) % group
                perm.append((b * tok_count + t, (group * t + s) * tok_count + b // group))
        row_blk = group * tok_index + (blk_index % group + d) % group
        on_diag = (row_blk == blk_index) & (col_ids == row_ids)
        gram = stacked[d, :, :span_width]
        reduced = jnp.where(on_diag, gram, OFF_SCALE * gram)
        bundle = jnp.concatenate([reduced, stacked[d, :, span_width:]], axis=1)
        pieces.append(lax.ppermute(bundle, ("blk", "tok"), perm))
    got = jnp.stack(pieces)
    order = (blk_index % group - jnp.arange(group)) % group
    got = jnp.take(got, order, axis=0)
    denominator = jnp.transpose(got[:, :, :span_width], (1, 0, 2)).reshape(ROW_DEV, group * span_width)
    numerator = jnp.transpose(got[:, :, span_width:], (1, 0, 2)).reshape(ROW_DEV, group * col_group)
    numerator = numerator + diag_term
    return (denominator, numerator)


def solution(mesh):
    placed = (P("mp", "tok", "blk"), P("mp", None, "blk"))
    return jax.shard_map(
        local,
        mesh=mesh,
        in_specs=placed,
        out_specs=(P("blk", "tok"), P("blk", "tok")),
        check_vma=False,
    )
```

```python
import jax
import jax.numpy as jnp
import numpy as np
from jax import lax
from jax.sharding import Mesh, PartitionSpec as P

ROW_DEV = 32


OFF_SCALE = 0.9


def local(inputs, down_weight):
    x_local = inputs[0]
    w_local = down_weight[0]
    tokens, span_width = x_local.shape
    cols = w_local.shape[0]
    hi_index = lax.axis_index("hi")
    lo_index = lax.axis_index("lo")
    tok_index = lax.axis_index("tok")
    group = lax.axis_size("lo")
    hi_count = lax.axis_size("hi")
    tok_count = lax.axis_size("tok")
    mp_count = lax.axis_size("mp")
    blk_count = hi_count * group
    col_group = cols // blk_count
    tok_cols = cols // tok_count

    y_part = lax.dot_general(
        x_local, w_local, (((1,), (1,)), ((), ())), preferred_element_type=jnp.float32
    )
    y_parts = lax.all_to_all(y_part, ("hi", "lo"), 1, 0, tiled=True)
    y_mine = jnp.sum(y_parts.reshape(blk_count, tokens, col_group), axis=0)
    y_round = lax.reduce_precision(y_mine, exponent_bits=8, mantissa_bits=7)
    y_high = y_round.astype(jnp.bfloat16)
    y_low = (y_mine - y_round).astype(jnp.bfloat16)

    win_lo = lax.all_gather(x_local[:, :ROW_DEV], "lo", axis=1, tiled=True)
    payload = jnp.concatenate([x_local, win_lo, y_high, y_low], axis=1)
    full = lax.all_gather(payload, "tok", axis=0, tiled=True)
    x_full = full[:, :span_width]
    win_end = span_width + group * ROW_DEV
    wins = full[:, span_width:win_end]
    y_tok = full[:, win_end:win_end + col_group].astype(jnp.float32) + full[:, win_end + col_group:].astype(jnp.float32)

    swap = [(h * tok_count + t, t * tok_count + h) for h in range(hi_count) for t in range(tok_count)]
    wins = lax.ppermute(wins, ("hi", "tok"), swap)

    gram = lax.dot_general(
        wins, x_full, (((0,), (0,)), ((), ())), preferred_element_type=jnp.float32
    )
    cross = lax.dot_general(
        wins.astype(jnp.float32), y_tok, (((0,), (0,)), ((), ())),
        precision=lax.Precision.HIGHEST, preferred_element_type=jnp.float32,
    )
    pieces = jnp.concatenate([gram, OFF_SCALE * cross], axis=1)
    pieces = lax.ppermute(pieces, ("hi", "tok"), swap)
    pieces = pieces.reshape(group, ROW_DEV, span_width + col_group)

    win_own = x_full[:, :ROW_DEV].astype(jnp.float32)
    diag = jnp.sum(win_own * win_own, axis=0)
    w_cols = lax.dynamic_slice_in_dim(w_local, tok_index * tok_cols, tok_cols, 0)
    diag_term = (1.0 - OFF_SCALE) * diag[:, None] * w_cols[:, :ROW_DEV].astype(jnp.float32).T
    is_self = (jnp.arange(group) == lo_index)[:, None, None]
    diag_part = jnp.where(is_self, diag_term[None], 0.0)

    send = jnp.concatenate([pieces, diag_part], axis=2)
    send = jnp.concatenate([send] * mp_count, axis=0)
    got = lax.all_to_all(send, ("mp", "lo"), 0, 0, tiled=True)
    got = jnp.sum(got.reshape(mp_count, group, ROW_DEV, -1), axis=0)

    gram = got[:, :, :span_width]
    slot = lax.broadcasted_iota(jnp.int32, gram.shape, 0)
    row_ids = lax.broadcasted_iota(jnp.int32, gram.shape, 1)
    col_ids = lax.broadcasted_iota(jnp.int32, gram.shape, 2)
    on_diag = (tok_index == hi_index) & (slot == lo_index) & (col_ids == row_ids)
    reduced = jnp.where(on_diag, gram, OFF_SCALE * gram)
    denominator = jnp.transpose(reduced, (1, 0, 2)).reshape(ROW_DEV, group * span_width)
    numerator = jnp.transpose(got[:, :, span_width:span_width + col_group], (1, 0, 2)).reshape(ROW_DEV, tok_cols)
    numerator = numerator + jnp.sum(got[:, :, span_width + col_group:], axis=0)
    return (denominator, numerator)


def solution(mesh):
    mp_count, blk_count, tok_count = (mesh.shape[a] for a in ("mp", "blk", "tok"))
    group = blk_count // tok_count
    devices = np.asarray(mesh.devices).reshape(mp_count, tok_count, group, tok_count)
    split = Mesh(devices, ("mp", "hi", "lo", "tok"))
    placed = (P("mp", "tok", ("hi", "lo")), P("mp", None, ("hi", "lo")))
    return jax.shard_map(
        local,
        mesh=split,
        in_specs=placed,
        out_specs=(P(("hi", "lo"), "tok"), P(("hi", "lo"), "tok")),
        check_vma=False,
    )
```

```python
import jax
import jax.numpy as jnp
import numpy as np
from jax import lax
from jax.sharding import Mesh, PartitionSpec as P

ROW_DEV = 32


OFF_SCALE = 0.9


def local(inputs, down_weight):
    x_local = inputs[0]
    w_local = down_weight[0]
    tokens, span_width = x_local.shape
    cols = w_local.shape[0]
    hi_index = lax.axis_index("hi")
    lo_index = lax.axis_index("lo")
    tok_index = lax.axis_index("tok")
    group = lax.axis_size("lo")
    hi_count = lax.axis_size("hi")
    tok_count = lax.axis_size("tok")
    mp_count = lax.axis_size("mp")
    blk_count = hi_count * group
    col_group = cols // blk_count
    tok_cols = cols // tok_count

    win_parts = lax.all_gather(x_local[:, :ROW_DEV], ("lo", "tok"), axis=0, tiled=False)
    wins = jnp.transpose(win_parts.reshape(group, tok_count, tokens, ROW_DEV), (1, 2, 0, 3))
    wins = wins.reshape(tok_count * tokens, group * ROW_DEV)

    swap = [(h * tok_count + t, t * tok_count + h) for h in range(hi_count) for t in range(tok_count)]
    x_swapped = lax.ppermute(x_local, ("hi", "tok"), swap)

    y_part = lax.dot_general(
        x_local, w_local, (((1,), (1,)), ((), ())), preferred_element_type=jnp.float32
    )
    y_parts = lax.all_to_all(y_part, ("hi", "lo"), 1, 0, tiled=True)
    y_mine = jnp.sum(y_parts.reshape(blk_count, tokens, col_group), axis=0)
    y_mine = lax.ppermute(y_mine, ("hi", "tok"), swap)
    y_round = lax.reduce_precision(y_mine, exponent_bits=8, mantissa_bits=7)
    y_high = y_round.astype(jnp.bfloat16)
    y_low = (y_mine - y_round).astype(jnp.bfloat16)

    payload = jnp.concatenate([x_swapped, y_high, y_low], axis=1)
    full = lax.all_gather(payload, "hi", axis=0, tiled=True)
    x_full = full[:, :span_width]
    y_tok = full[:, span_width:span_width + col_group].astype(jnp.float32) + full[:, span_width + col_group:].astype(jnp.float32)

    gram = lax.dot_general(
        wins, x_full, (((0,), (0,)), ((), ())), preferred_element_type=jnp.float32
    )
    cross = lax.dot_general(
        wins.astype(jnp.float32), y_tok, (((0,), (0,)), ((), ())),
        precision=lax.Precision.HIGHEST, preferred_element_type=jnp.float32,
    )
    pieces = jnp.concatenate([gram, OFF_SCALE * cross], axis=1)
    pieces = pieces.reshape(group, ROW_DEV, span_width + col_group)

    win_own = lax.dynamic_slice_in_dim(wins, lo_index * ROW_DEV, ROW_DEV, 1).astype(jnp.float32)
    diag = jnp.sum(win_own * win_own, axis=0)
    w_cols = lax.dynamic_slice_in_dim(w_local, tok_index * tok_cols, tok_cols, 0)
    diag_term = (1.0 - OFF_SCALE) * diag[:, None] * w_cols[:, :ROW_DEV].astype(jnp.float32).T
    is_self = (jnp.arange(group) == lo_index)[:, None, None]
    diag_part = jnp.where(is_self, diag_term[None], 0.0)

    send = jnp.concatenate([pieces, diag_part], axis=2)
    send = jnp.concatenate([send] * mp_count, axis=0)
    got = lax.all_to_all(send, ("mp", "lo"), 0, 0, tiled=True)
    got = jnp.sum(got.reshape(mp_count, group, ROW_DEV, -1), axis=0)

    gram = got[:, :, :span_width]
    slot = lax.broadcasted_iota(jnp.int32, gram.shape, 0)
    row_ids = lax.broadcasted_iota(jnp.int32, gram.shape, 1)
    col_ids = lax.broadcasted_iota(jnp.int32, gram.shape, 2)
    on_diag = (tok_index == hi_index) & (slot == lo_index) & (col_ids == row_ids)
    reduced = jnp.where(on_diag, gram, OFF_SCALE * gram)
    denominator = jnp.transpose(reduced, (1, 0, 2)).reshape(ROW_DEV, group * span_width)
    numerator = jnp.transpose(got[:, :, span_width:span_width + col_group], (1, 0, 2)).reshape(ROW_DEV, tok_cols)
    numerator = numerator + jnp.sum(got[:, :, span_width + col_group:], axis=0)
    return (denominator, numerator)


def solution(mesh):
    mp_count, blk_count, tok_count = (mesh.shape[a] for a in ("mp", "blk", "tok"))
    group = blk_count // tok_count
    devices = np.asarray(mesh.devices).reshape(mp_count, tok_count, group, tok_count)
    split = Mesh(devices, ("mp", "hi", "lo", "tok"))
    placed = (P("mp", "tok", ("hi", "lo")), P("mp", None, ("hi", "lo")))
    return jax.shard_map(
        local,
        mesh=split,
        in_specs=placed,
        out_specs=(P(("hi", "lo"), "tok"), P(("hi", "lo"), "tok")),
        check_vma=False,
    )
```

```python
import jax
import jax.numpy as jnp
import numpy as np
from jax import lax
from jax.sharding import Mesh, PartitionSpec as P

ROW_DEV = 32


OFF_SCALE = 0.9


def local(inputs, down_weight):
    x_local = inputs[0]
    w_local = down_weight[0]
    tokens, span_width = x_local.shape
    cols = w_local.shape[0]
    hi_index = lax.axis_index("hi")
    lo_index = lax.axis_index("lo")
    tok_index = lax.axis_index("tok")
    group = lax.axis_size("lo")
    hi_count = lax.axis_size("hi")
    tok_count = lax.axis_size("tok")
    mp_count = lax.axis_size("mp")
    blk_count = hi_count * group
    col_group = cols // blk_count
    tok_cols = cols // tok_count

    win_lo = lax.all_gather(x_local[:, :ROW_DEV], "lo", axis=1, tiled=True)
    wins = lax.all_gather(win_lo, "tok", axis=0, tiled=True)

    swap = [(h * tok_count + t, t * tok_count + h) for h in range(hi_count) for t in range(tok_count)]
    x_swapped = lax.ppermute(x_local, ("hi", "tok"), swap)

    y_part = lax.dot_general(
        x_local, w_local, (((1,), (1,)), ((), ())), preferred_element_type=jnp.float32
    )
    y_parts = lax.all_to_all(y_part, ("hi", "lo"), 1, 0, tiled=True)
    y_mine = jnp.sum(y_parts.reshape(blk_count, tokens, col_group), axis=0)
    y_mine = lax.ppermute(y_mine, ("hi", "tok"), swap)
    y_round = lax.reduce_precision(y_mine, exponent_bits=8, mantissa_bits=7)
    y_high = y_round.astype(jnp.bfloat16)
    y_low = (y_mine - y_round).astype(jnp.bfloat16)

    payload = jnp.concatenate([x_swapped, y_high, y_low], axis=1)
    full = lax.all_gather(payload, "hi", axis=0, tiled=True)
    x_full = full[:, :span_width]
    y_tok = full[:, span_width:span_width + col_group].astype(jnp.float32) + full[:, span_width + col_group:].astype(jnp.float32)

    gram = lax.dot_general(
        wins, x_full, (((0,), (0,)), ((), ())), preferred_element_type=jnp.float32
    )
    cross = lax.dot_general(
        wins.astype(jnp.float32), y_tok, (((0,), (0,)), ((), ())),
        precision=lax.Precision.HIGHEST, preferred_element_type=jnp.float32,
    )
    pieces = jnp.concatenate([gram, OFF_SCALE * cross], axis=1)
    pieces = pieces.reshape(group, ROW_DEV, span_width + col_group)

    win_own = lax.dynamic_slice_in_dim(wins, lo_index * ROW_DEV, ROW_DEV, 1).astype(jnp.float32)
    diag = jnp.sum(win_own * win_own, axis=0)
    w_cols = lax.dynamic_slice_in_dim(w_local, tok_index * tok_cols, tok_cols, 0)
    diag_term = (1.0 - OFF_SCALE) * diag[:, None] * w_cols[:, :ROW_DEV].astype(jnp.float32).T
    is_self = (jnp.arange(group) == lo_index)[:, None, None]
    diag_part = jnp.where(is_self, diag_term[None], 0.0)

    send = jnp.concatenate([pieces, diag_part], axis=2)
    send = jnp.concatenate([send] * mp_count, axis=0)
    got = lax.all_to_all(send, ("mp", "lo"), 0, 0, tiled=True)
    got = jnp.sum(got.reshape(mp_count, group, ROW_DEV, -1), axis=0)

    gram = got[:, :, :span_width]
    slot = lax.broadcasted_iota(jnp.int32, gram.shape, 0)
    row_ids = lax.broadcasted_iota(jnp.int32, gram.shape, 1)
    col_ids = lax.broadcasted_iota(jnp.int32, gram.shape, 2)
    on_diag = (tok_index == hi_index) & (slot == lo_index) & (col_ids == row_ids)
    reduced = jnp.where(on_diag, gram, OFF_SCALE * gram)
    denominator = jnp.transpose(reduced, (1, 0, 2)).reshape(ROW_DEV, group * span_width)
    numerator = jnp.transpose(got[:, :, span_width:span_width + col_group], (1, 0, 2)).reshape(ROW_DEV, tok_cols)
    numerator = numerator + jnp.sum(got[:, :, span_width + col_group:], axis=0)
    return (denominator, numerator)


def solution(mesh):
    mp_count, blk_count, tok_count = (mesh.shape[a] for a in ("mp", "blk", "tok"))
    group = blk_count // tok_count
    devices = np.asarray(mesh.devices).reshape(mp_count, tok_count, group, tok_count)
    split = Mesh(devices, ("mp", "hi", "lo", "tok"))
    placed = (P("mp", "tok", ("hi", "lo")), P("mp", None, ("hi", "lo")))
    return jax.shard_map(
        local,
        mesh=split,
        in_specs=placed,
        out_specs=(P(("hi", "lo"), "tok"), P(("hi", "lo"), "tok")),
        check_vma=False,
    )
```

```python
import jax
import jax.numpy as jnp
import numpy as np
from jax import lax
from jax.sharding import Mesh, PartitionSpec as P

ROW_DEV = 32


OFF_SCALE = 0.9


def local(inputs, down_weight):
    x_local = inputs[0]
    w_local = down_weight[0]
    tokens, span_width = x_local.shape
    cols = w_local.shape[0]
    hi_index = lax.axis_index("hi")
    lo_index = lax.axis_index("lo")
    tok_index = lax.axis_index("tok")
    group = lax.axis_size("lo")
    hi_count = lax.axis_size("hi")
    tok_count = lax.axis_size("tok")
    mp_count = lax.axis_size("mp")
    blk_count = hi_count * group
    col_group = cols // blk_count
    tok_cols = cols // tok_count

    win_lo = lax.all_gather(x_local[:, :ROW_DEV], "lo", axis=1, tiled=True)
    wins = lax.all_gather(win_lo, "tok", axis=0, tiled=True)

    swap = [(h * tok_count + t, t * tok_count + h) for h in range(hi_count) for t in range(tok_count)]
    x_swapped = lax.ppermute(x_local, ("hi", "tok"), swap)

    y_part = lax.dot_general(
        x_local, w_local, (((1,), (1,)), ((), ())), preferred_element_type=jnp.float32
    )
    y_parts = lax.all_to_all(y_part, ("hi", "lo"), 1, 0, tiled=True)
    y_mine = jnp.sum(y_parts.reshape(blk_count, tokens, col_group), axis=0)
    y_mine = lax.ppermute(y_mine, ("hi", "tok"), swap)
    y_round = lax.reduce_precision(y_mine, exponent_bits=8, mantissa_bits=7)
    y_high = y_round.astype(jnp.bfloat16)
    y_low = (y_mine - y_round).astype(jnp.bfloat16)

    payload = jnp.concatenate([x_swapped, y_high, y_low], axis=1)
    spread = jnp.broadcast_to(payload[None], (hi_count,) + payload.shape)
    full = lax.all_to_all(spread, "hi", 0, 0, tiled=True).reshape(hi_count * tokens, -1)
    x_full = full[:, :span_width]
    y_tok = full[:, span_width:span_width + col_group].astype(jnp.float32) + full[:, span_width + col_group:].astype(jnp.float32)

    gram = lax.dot_general(
        wins, x_full, (((0,), (0,)), ((), ())), preferred_element_type=jnp.float32
    )
    cross = lax.dot_general(
        wins.astype(jnp.float32), y_tok, (((0,), (0,)), ((), ())),
        precision=lax.Precision.HIGHEST, preferred_element_type=jnp.float32,
    )
    pieces = jnp.concatenate([gram, OFF_SCALE * cross], axis=1)
    pieces = pieces.reshape(group, ROW_DEV, span_width + col_group)

    win_own = lax.dynamic_slice_in_dim(wins, lo_index * ROW_DEV, ROW_DEV, 1).astype(jnp.float32)
    diag = jnp.sum(win_own * win_own, axis=0)
    w_cols = lax.dynamic_slice_in_dim(w_local, tok_index * tok_cols, tok_cols, 0)
    diag_term = (1.0 - OFF_SCALE) * diag[:, None] * w_cols[:, :ROW_DEV].astype(jnp.float32).T
    is_self = (jnp.arange(group) == lo_index)[:, None, None]
    diag_part = jnp.where(is_self, diag_term[None], 0.0)

    send = jnp.concatenate([pieces, diag_part], axis=2)
    send = jnp.concatenate([send] * mp_count, axis=0)
    got = lax.all_to_all(send, ("mp", "lo"), 0, 0, tiled=True)
    got = jnp.sum(got.reshape(mp_count, group, ROW_DEV, -1), axis=0)

    gram = got[:, :, :span_width]
    slot = lax.broadcasted_iota(jnp.int32, gram.shape, 0)
    row_ids = lax.broadcasted_iota(jnp.int32, gram.shape, 1)
    col_ids = lax.broadcasted_iota(jnp.int32, gram.shape, 2)
    on_diag = (tok_index == hi_index) & (slot == lo_index) & (col_ids == row_ids)
    reduced = jnp.where(on_diag, gram, OFF_SCALE * gram)
    denominator = jnp.transpose(reduced, (1, 0, 2)).reshape(ROW_DEV, group * span_width)
    numerator = jnp.transpose(got[:, :, span_width:span_width + col_group], (1, 0, 2)).reshape(ROW_DEV, tok_cols)
    numerator = numerator + jnp.sum(got[:, :, span_width + col_group:], axis=0)
    return (denominator, numerator)


def solution(mesh):
    mp_count, blk_count, tok_count = (mesh.shape[a] for a in ("mp", "blk", "tok"))
    group = blk_count // tok_count
    devices = np.asarray(mesh.devices).reshape(mp_count, tok_count, group, tok_count)
    split = Mesh(devices, ("mp", "hi", "lo", "tok"))
    placed = (P("mp", "tok", ("hi", "lo")), P("mp", None, ("hi", "lo")))
    return jax.shard_map(
        local,
        mesh=split,
        in_specs=placed,
        out_specs=(P(("hi", "lo"), "tok"), P(("hi", "lo"), "tok")),
        check_vma=False,
    )
```

```python
import jax
import jax.numpy as jnp
import numpy as np
from jax import lax
from jax.sharding import Mesh, PartitionSpec as P

ROW_DEV = 32


OFF_SCALE = 0.9


def local(inputs, down_weight):
    x_local = inputs[0]
    w_local = down_weight[0]
    tokens, span_width = x_local.shape
    cols = w_local.shape[0]
    hi_index = lax.axis_index("hi")
    lo_index = lax.axis_index("lo")
    tok_index = lax.axis_index("tok")
    group = lax.axis_size("lo")
    hi_count = lax.axis_size("hi")
    tok_count = lax.axis_size("tok")
    mp_count = lax.axis_size("mp")
    blk_count = hi_count * group
    col_group = cols // blk_count
    tok_cols = cols // tok_count

    win_lo = lax.all_gather(x_local[:, :ROW_DEV], "lo", axis=1, tiled=True)
    wins = lax.all_gather(win_lo, "tok", axis=0, tiled=True)
    x_local, w_local, wins = lax.optimization_barrier((x_local, w_local, wins))

    swap = [(h * tok_count + t, t * tok_count + h) for h in range(hi_count) for t in range(tok_count)]
    x_swapped = lax.ppermute(x_local, ("hi", "tok"), swap)

    y_part = lax.dot_general(
        x_local, w_local, (((1,), (1,)), ((), ())), preferred_element_type=jnp.float32
    )
    y_parts = lax.all_to_all(y_part, ("hi", "lo"), 1, 0, tiled=True)
    y_mine = jnp.sum(y_parts.reshape(blk_count, tokens, col_group), axis=0)
    y_mine = lax.ppermute(y_mine, ("hi", "tok"), swap)
    y_round = lax.reduce_precision(y_mine, exponent_bits=8, mantissa_bits=7)
    y_high = y_round.astype(jnp.bfloat16)
    y_low = (y_mine - y_round).astype(jnp.bfloat16)

    payload = jnp.concatenate([x_swapped, y_high, y_low], axis=1)
    spread = jnp.broadcast_to(payload[None], (hi_count,) + payload.shape)
    full = lax.all_to_all(spread, "hi", 0, 0, tiled=True).reshape(hi_count * tokens, -1)
    x_full = full[:, :span_width]
    y_tok = full[:, span_width:span_width + col_group].astype(jnp.float32) + full[:, span_width + col_group:].astype(jnp.float32)

    gram = lax.dot_general(
        wins, x_full, (((0,), (0,)), ((), ())), preferred_element_type=jnp.float32
    )
    cross = lax.dot_general(
        wins.astype(jnp.float32), y_tok, (((0,), (0,)), ((), ())),
        precision=lax.Precision.HIGHEST, preferred_element_type=jnp.float32,
    )
    pieces = jnp.concatenate([gram, OFF_SCALE * cross], axis=1)
    pieces = pieces.reshape(group, ROW_DEV, span_width + col_group)

    win_own = lax.dynamic_slice_in_dim(wins, lo_index * ROW_DEV, ROW_DEV, 1).astype(jnp.float32)
    diag = jnp.sum(win_own * win_own, axis=0)
    w_cols = lax.dynamic_slice_in_dim(w_local, tok_index * tok_cols, tok_cols, 0)
    diag_term = (1.0 - OFF_SCALE) * diag[:, None] * w_cols[:, :ROW_DEV].astype(jnp.float32).T
    is_self = (jnp.arange(group) == lo_index)[:, None, None]
    diag_part = jnp.where(is_self, diag_term[None], 0.0)

    send = jnp.concatenate([pieces, diag_part], axis=2)
    send = jnp.concatenate([send] * mp_count, axis=0)
    got = lax.all_to_all(send, ("mp", "lo"), 0, 0, tiled=True)
    got = jnp.sum(got.reshape(mp_count, group, ROW_DEV, -1), axis=0)

    gram = got[:, :, :span_width]
    slot = lax.broadcasted_iota(jnp.int32, gram.shape, 0)
    row_ids = lax.broadcasted_iota(jnp.int32, gram.shape, 1)
    col_ids = lax.broadcasted_iota(jnp.int32, gram.shape, 2)
    on_diag = (tok_index == hi_index) & (slot == lo_index) & (col_ids == row_ids)
    reduced = jnp.where(on_diag, gram, OFF_SCALE * gram)
    denominator = jnp.transpose(reduced, (1, 0, 2)).reshape(ROW_DEV, group * span_width)
    numerator = jnp.transpose(got[:, :, span_width:span_width + col_group], (1, 0, 2)).reshape(ROW_DEV, tok_cols)
    numerator = numerator + jnp.sum(got[:, :, span_width + col_group:], axis=0)
    return (denominator, numerator)


def solution(mesh):
    mp_count, blk_count, tok_count = (mesh.shape[a] for a in ("mp", "blk", "tok"))
    group = blk_count // tok_count
    devices = np.asarray(mesh.devices).reshape(mp_count, tok_count, group, tok_count)
    split = Mesh(devices, ("mp", "hi", "lo", "tok"))
    placed = (P("mp", "tok", ("hi", "lo")), P("mp", None, ("hi", "lo")))
    return jax.shard_map(
        local,
        mesh=split,
        in_specs=placed,
        out_specs=(P(("hi", "lo"), "tok"), P(("hi", "lo"), "tok")),
        check_vma=False,
    )
```

```python
import jax
import jax.numpy as jnp
import numpy as np
from jax import lax
from jax.experimental import pallas as pl
from jax.experimental.pallas import tpu as pltpu
from jax.sharding import Mesh, PartitionSpec as P

ROW_DEV = 32


OFF_SCALE = 0.9


def _pieces_kernel(span_width, col_group, win_ref, full_ref, out_ref):
    wins = win_ref[...]
    x_full = full_ref[:, :span_width]
    y_tok = (full_ref[:, span_width:span_width + col_group].astype(jnp.float32)
             + full_ref[:, span_width + col_group:].astype(jnp.float32))
    out_ref[:, :span_width] = lax.dot_general(
        wins, x_full, (((0,), (0,)), ((), ())), preferred_element_type=jnp.float32
    )
    cross = lax.dot_general(
        wins.astype(jnp.float32), y_tok, (((0,), (0,)), ((), ())),
        precision=lax.Precision.HIGHEST, preferred_element_type=jnp.float32,
    )
    out_ref[:, span_width:] = OFF_SCALE * cross


def window_pieces(wins, full, span_width, col_group):
    rows = wins.shape[1]
    return pl.pallas_call(
        lambda *refs: _pieces_kernel(span_width, col_group, *refs),
        out_shape=jax.ShapeDtypeStruct((rows, span_width + col_group), jnp.float32),
        in_specs=[pl.BlockSpec(memory_space=pltpu.VMEM)] * 2,
        out_specs=pl.BlockSpec(memory_space=pltpu.VMEM),
    )(wins, full)


def local(inputs, down_weight):
    x_local = inputs[0]
    w_local = down_weight[0]
    tokens, span_width = x_local.shape
    cols = w_local.shape[0]
    hi_index = lax.axis_index("hi")
    lo_index = lax.axis_index("lo")
    tok_index = lax.axis_index("tok")
    group = lax.axis_size("lo")
    hi_count = lax.axis_size("hi")
    tok_count = lax.axis_size("tok")
    mp_count = lax.axis_size("mp")
    blk_count = hi_count * group
    col_group = cols // blk_count
    tok_cols = cols // tok_count

    win_lo = lax.all_gather(x_local[:, :ROW_DEV], "lo", axis=1, tiled=True)
    wins = lax.all_gather(win_lo, "tok", axis=0, tiled=True)

    swap = [(h * tok_count + t, t * tok_count + h) for h in range(hi_count) for t in range(tok_count)]
    x_swapped = lax.ppermute(x_local, ("hi", "tok"), swap)

    y_part = lax.dot_general(
        x_local, w_local, (((1,), (1,)), ((), ())), preferred_element_type=jnp.float32
    )
    y_parts = lax.all_to_all(y_part, ("hi", "lo"), 1, 0, tiled=True)
    y_mine = jnp.sum(y_parts.reshape(blk_count, tokens, col_group), axis=0)
    y_mine = lax.ppermute(y_mine, ("hi", "tok"), swap)
    y_round = lax.reduce_precision(y_mine, exponent_bits=8, mantissa_bits=7)
    y_high = y_round.astype(jnp.bfloat16)
    y_low = (y_mine - y_round).astype(jnp.bfloat16)

    payload = jnp.concatenate([x_swapped, y_high, y_low], axis=1)
    spread = jnp.broadcast_to(payload[None], (hi_count,) + payload.shape)
    full = lax.all_to_all(spread, "hi", 0, 0, tiled=True).reshape(hi_count * tokens, -1)
    pieces = window_pieces(wins, full, span_width, col_group)
    pieces = pieces.reshape(group, ROW_DEV, span_width + col_group)

    win_own = lax.dynamic_slice_in_dim(wins, lo_index * ROW_DEV, ROW_DEV, 1).astype(jnp.float32)
    diag = jnp.sum(win_own * win_own, axis=0)
    w_cols = lax.dynamic_slice_in_dim(w_local, tok_index * tok_cols, tok_cols, 0)
    diag_term = (1.0 - OFF_SCALE) * diag[:, None] * w_cols[:, :ROW_DEV].astype(jnp.float32).T
    is_self = (jnp.arange(group) == lo_index)[:, None, None]
    diag_part = jnp.where(is_self, diag_term[None], 0.0)

    send = jnp.concatenate([pieces, diag_part], axis=2)
    send = jnp.concatenate([send] * mp_count, axis=0)
    got = lax.all_to_all(send, ("mp", "lo"), 0, 0, tiled=True)
    got = jnp.sum(got.reshape(mp_count, group, ROW_DEV, -1), axis=0)

    gram = got[:, :, :span_width]
    slot = lax.broadcasted_iota(jnp.int32, gram.shape, 0)
    row_ids = lax.broadcasted_iota(jnp.int32, gram.shape, 1)
    col_ids = lax.broadcasted_iota(jnp.int32, gram.shape, 2)
    on_diag = (tok_index == hi_index) & (slot == lo_index) & (col_ids == row_ids)
    reduced = jnp.where(on_diag, gram, OFF_SCALE * gram)
    denominator = jnp.transpose(reduced, (1, 0, 2)).reshape(ROW_DEV, group * span_width)
    numerator = jnp.transpose(got[:, :, span_width:span_width + col_group], (1, 0, 2)).reshape(ROW_DEV, tok_cols)
    numerator = numerator + jnp.sum(got[:, :, span_width + col_group:], axis=0)
    return (denominator, numerator)


def solution(mesh):
    mp_count, blk_count, tok_count = (mesh.shape[a] for a in ("mp", "blk", "tok"))
    group = blk_count // tok_count
    devices = np.asarray(mesh.devices).reshape(mp_count, tok_count, group, tok_count)
    split = Mesh(devices, ("mp", "hi", "lo", "tok"))
    placed = (P("mp", "tok", ("hi", "lo")), P("mp", None, ("hi", "lo")))
    return jax.shard_map(
        local,
        mesh=split,
        in_specs=placed,
        out_specs=(P(("hi", "lo"), "tok"), P(("hi", "lo"), "tok")),
        check_vma=False,
    )
```

```python
import jax
import jax.numpy as jnp
import numpy as np
from jax import lax
from jax.sharding import Mesh, PartitionSpec as P

ROW_DEV = 32


OFF_SCALE = 0.9


def local(inputs, down_weight):
    x_local = inputs[0]
    w_local = down_weight[0]
    tokens, span_width = x_local.shape
    cols = w_local.shape[0]
    hi_index = lax.axis_index("hi")
    lo_index = lax.axis_index("lo")
    tok_index = lax.axis_index("tok")
    group = lax.axis_size("lo")
    hi_count = lax.axis_size("hi")
    tok_count = lax.axis_size("tok")
    mp_count = lax.axis_size("mp")
    blk_count = hi_count * group
    col_group = cols // blk_count
    tok_cols = cols // tok_count

    win_lo = lax.all_gather(x_local[:, :ROW_DEV], "lo", axis=1, tiled=True)
    wins = lax.all_gather(win_lo, "tok", axis=0, tiled=True)

    swap = [(h * tok_count + t, t * tok_count + h) for h in range(hi_count) for t in range(tok_count)]
    x_swapped = lax.ppermute(x_local, ("hi", "tok"), swap)

    y_part = lax.dot_general(
        x_local, w_local, (((1,), (1,)), ((), ())), preferred_element_type=jnp.float32
    )
    y_parts = lax.all_to_all(y_part, ("hi", "lo"), 1, 0, tiled=True)
    y_mine = jnp.sum(y_parts.reshape(blk_count, tokens, col_group), axis=0)
    y_mine = lax.ppermute(y_mine, ("hi", "tok"), swap)
    y_round = lax.reduce_precision(y_mine, exponent_bits=8, mantissa_bits=7)
    y_high = y_round.astype(jnp.bfloat16)
    y_low = (y_mine - y_round).astype(jnp.bfloat16)

    payload = jnp.concatenate([x_swapped, y_high, y_low], axis=1)
    half = span_width // 2
    first = lax.all_gather(payload[:, :half], "hi", axis=0, tiled=True)
    rest = payload[:, half:]
    spread = jnp.broadcast_to(rest[None], (hi_count,) + rest.shape)
    second = lax.all_to_all(spread, "hi", 0, 0, tiled=True).reshape(hi_count * tokens, -1)
    full = jnp.concatenate([first, second], axis=1)
    x_full = full[:, :span_width]
    y_tok = full[:, span_width:span_width + col_group].astype(jnp.float32) + full[:, span_width + col_group:].astype(jnp.float32)

    gram = lax.dot_general(
        wins, x_full, (((0,), (0,)), ((), ())), preferred_element_type=jnp.float32
    )
    cross = lax.dot_general(
        wins.astype(jnp.float32), y_tok, (((0,), (0,)), ((), ())),
        precision=lax.Precision.HIGHEST, preferred_element_type=jnp.float32,
    )
    pieces = jnp.concatenate([gram, OFF_SCALE * cross], axis=1)
    pieces = pieces.reshape(group, ROW_DEV, span_width + col_group)

    win_own = lax.dynamic_slice_in_dim(wins, lo_index * ROW_DEV, ROW_DEV, 1).astype(jnp.float32)
    diag = jnp.sum(win_own * win_own, axis=0)
    w_cols = lax.dynamic_slice_in_dim(w_local, tok_index * tok_cols, tok_cols, 0)
    diag_term = (1.0 - OFF_SCALE) * diag[:, None] * w_cols[:, :ROW_DEV].astype(jnp.float32).T
    is_self = (jnp.arange(group) == lo_index)[:, None, None]
    diag_part = jnp.where(is_self, diag_term[None], 0.0)

    send = jnp.concatenate([pieces, diag_part], axis=2)
    send = jnp.concatenate([send] * mp_count, axis=0)
    got = lax.all_to_all(send, ("mp", "lo"), 0, 0, tiled=True)
    got = jnp.sum(got.reshape(mp_count, group, ROW_DEV, -1), axis=0)

    gram = got[:, :, :span_width]
    slot = lax.broadcasted_iota(jnp.int32, gram.shape, 0)
    row_ids = lax.broadcasted_iota(jnp.int32, gram.shape, 1)
    col_ids = lax.broadcasted_iota(jnp.int32, gram.shape, 2)
    on_diag = (tok_index == hi_index) & (slot == lo_index) & (col_ids == row_ids)
    reduced = jnp.where(on_diag, gram, OFF_SCALE * gram)
    denominator = jnp.transpose(reduced, (1, 0, 2)).reshape(ROW_DEV, group * span_width)
    numerator = jnp.transpose(got[:, :, span_width:span_width + col_group], (1, 0, 2)).reshape(ROW_DEV, tok_cols)
    numerator = numerator + jnp.sum(got[:, :, span_width + col_group:], axis=0)
    return (denominator, numerator)


def solution(mesh):
    mp_count, blk_count, tok_count = (mesh.shape[a] for a in ("mp", "blk", "tok"))
    group = blk_count // tok_count
    devices = np.asarray(mesh.devices).reshape(mp_count, tok_count, group, tok_count)
    split = Mesh(devices, ("mp", "hi", "lo", "tok"))
    placed = (P("mp", "tok", ("hi", "lo")), P("mp", None, ("hi", "lo")))
    return jax.shard_map(
        local,
        mesh=split,
        in_specs=placed,
        out_specs=(P(("hi", "lo"), "tok"), P(("hi", "lo"), "tok")),
        check_vma=False,
    )
```

```python
import jax
import jax.numpy as jnp
import numpy as np
from jax import lax
from jax.sharding import Mesh, PartitionSpec as P

ROW_DEV = 32


OFF_SCALE = 0.9


def local(inputs, down_weight):
    x_local = inputs[0]
    w_local = down_weight[0]
    tokens, span_width = x_local.shape
    cols = w_local.shape[0]
    hi_index = lax.axis_index("hi")
    lo_index = lax.axis_index("lo")
    tok_index = lax.axis_index("tok")
    group = lax.axis_size("lo")
    hi_count = lax.axis_size("hi")
    tok_count = lax.axis_size("tok")
    mp_count = lax.axis_size("mp")
    blk_count = hi_count * group
    col_group = cols // blk_count
    tok_cols = cols // tok_count

    win_lo = lax.all_gather(x_local[:, :ROW_DEV], "lo", axis=1, tiled=True)
    wins = lax.all_gather(win_lo, "tok", axis=0, tiled=True)

    swap = [(h * tok_count + t, t * tok_count + h) for h in range(hi_count) for t in range(tok_count)]
    x_swapped = lax.ppermute(x_local, ("hi", "tok"), swap)

    x_for_y, w_for_y, wins, x_swapped = lax.optimization_barrier((x_local, w_local, wins, x_swapped))
    y_part = lax.dot_general(
        x_for_y, w_for_y, (((1,), (1,)), ((), ())), preferred_element_type=jnp.float32
    )
    y_parts = lax.all_to_all(y_part, ("hi", "lo"), 1, 0, tiled=True)
    y_mine = jnp.sum(y_parts.reshape(blk_count, tokens, col_group), axis=0)
    y_mine = lax.ppermute(y_mine, ("hi", "tok"), swap)
    y_round = lax.reduce_precision(y_mine, exponent_bits=8, mantissa_bits=7)
    y_high = y_round.astype(jnp.bfloat16)
    y_low = (y_mine - y_round).astype(jnp.bfloat16)

    payload = jnp.concatenate([x_swapped, y_high, y_low], axis=1)
    spread = jnp.broadcast_to(payload[None], (hi_count,) + payload.shape)
    full = lax.all_to_all(spread, "hi", 0, 0, tiled=True).reshape(hi_count * tokens, -1)
    x_full = full[:, :span_width]
    y_tok = full[:, span_width:span_width + col_group].astype(jnp.float32) + full[:, span_width + col_group:].astype(jnp.float32)

    gram = lax.dot_general(
        wins, x_full, (((0,), (0,)), ((), ())), preferred_element_type=jnp.float32
    )
    cross = lax.dot_general(
        wins.astype(jnp.float32), y_tok, (((0,), (0,)), ((), ())),
        precision=lax.Precision.HIGHEST, preferred_element_type=jnp.float32,
    )
    pieces = jnp.concatenate([gram, OFF_SCALE * cross], axis=1)
    pieces = pieces.reshape(group, ROW_DEV, span_width + col_group)

    win_own = lax.dynamic_slice_in_dim(wins, lo_index * ROW_DEV, ROW_DEV, 1).astype(jnp.float32)
    diag = jnp.sum(win_own * win_own, axis=0)
    w_cols = lax.dynamic_slice_in_dim(w_local, tok_index * tok_cols, tok_cols, 0)
    diag_term = (1.0 - OFF_SCALE) * diag[:, None] * w_cols[:, :ROW_DEV].astype(jnp.float32).T
    is_self = (jnp.arange(group) == lo_index)[:, None, None]
    diag_part = jnp.where(is_self, diag_term[None], 0.0)

    send = jnp.concatenate([pieces, diag_part], axis=2)
    send = jnp.concatenate([send] * mp_count, axis=0)
    got = lax.all_to_all(send, ("mp", "lo"), 0, 0, tiled=True)
    got = jnp.sum(got.reshape(mp_count, group, ROW_DEV, -1), axis=0)

    gram = got[:, :, :span_width]
    slot = lax.broadcasted_iota(jnp.int32, gram.shape, 0)
    row_ids = lax.broadcasted_iota(jnp.int32, gram.shape, 1)
    col_ids = lax.broadcasted_iota(jnp.int32, gram.shape, 2)
    on_diag = (tok_index == hi_index) & (slot == lo_index) & (col_ids == row_ids)
    reduced = jnp.where(on_diag, gram, OFF_SCALE * gram)
    denominator = jnp.transpose(reduced, (1, 0, 2)).reshape(ROW_DEV, group * span_width)
    numerator = jnp.transpose(got[:, :, span_width:span_width + col_group], (1, 0, 2)).reshape(ROW_DEV, tok_cols)
    numerator = numerator + jnp.sum(got[:, :, span_width + col_group:], axis=0)
    return (denominator, numerator)


def solution(mesh):
    mp_count, blk_count, tok_count = (mesh.shape[a] for a in ("mp", "blk", "tok"))
    group = blk_count // tok_count
    devices = np.asarray(mesh.devices).reshape(mp_count, tok_count, group, tok_count)
    split = Mesh(devices, ("mp", "hi", "lo", "tok"))
    placed = (P("mp", "tok", ("hi", "lo")), P("mp", None, ("hi", "lo")))
    return jax.shard_map(
        local,
        mesh=split,
        in_specs=placed,
        out_specs=(P(("hi", "lo"), "tok"), P(("hi", "lo"), "tok")),
        check_vma=False,
    )
```

```python
import jax
import jax.numpy as jnp
import numpy as np
from jax import lax
from jax.sharding import Mesh, PartitionSpec as P

ROW_DEV = 32


OFF_SCALE = 0.9


def local(inputs, down_weight):
    x_local = inputs[0]
    w_local = down_weight[0]
    tokens, span_width = x_local.shape
    cols = w_local.shape[0]
    hi_index = lax.axis_index("hi")
    lo_index = lax.axis_index("lo")
    tok_index = lax.axis_index("tok")
    group = lax.axis_size("lo")
    hi_count = lax.axis_size("hi")
    tok_count = lax.axis_size("tok")
    mp_count = lax.axis_size("mp")
    blk_count = hi_count * group
    col_group = cols // blk_count
    tok_cols = cols // tok_count

    win_lo = lax.all_gather(x_local[:, :ROW_DEV], "lo", axis=1, tiled=True)
    wins = lax.all_gather(win_lo, "tok", axis=0, tiled=True)

    swap = [(h * tok_count + t, t * tok_count + h) for h in range(hi_count) for t in range(tok_count)]
    x_swapped = lax.ppermute(x_local, ("hi", "tok"), swap)

    x_for_y, w_for_y, wins, x_swapped = lax.optimization_barrier((x_local, w_local, wins, x_swapped))
    spread = jnp.broadcast_to(x_swapped[None], (hi_count,) + x_swapped.shape)
    x_full = lax.all_to_all(spread, "hi", 0, 0, tiled=True).reshape(hi_count * tokens, span_width)
    y_part = lax.dot_general(
        x_for_y, w_for_y, (((1,), (1,)), ((), ())), preferred_element_type=jnp.float32
    )
    y_parts = lax.all_to_all(y_part, ("hi", "lo"), 1, 0, tiled=True)
    y_mine = jnp.sum(y_parts.reshape(blk_count, tokens, col_group), axis=0)
    y_mine = lax.ppermute(y_mine, ("hi", "tok"), swap)
    y_round = lax.reduce_precision(y_mine, exponent_bits=8, mantissa_bits=7)
    y_high = y_round.astype(jnp.bfloat16)
    y_low = (y_mine - y_round).astype(jnp.bfloat16)

    y_pair = jnp.concatenate([y_high, y_low], axis=1)
    y_spread = jnp.broadcast_to(y_pair[None], (hi_count,) + y_pair.shape)
    y_pair = lax.all_to_all(y_spread, "hi", 0, 0, tiled=True).reshape(hi_count * tokens, -1)
    y_tok = y_pair[:, :col_group].astype(jnp.float32) + y_pair[:, col_group:].astype(jnp.float32)

    gram = lax.dot_general(
        wins, x_full, (((0,), (0,)), ((), ())), preferred_element_type=jnp.float32
    )
    cross = lax.dot_general(
        wins.astype(jnp.float32), y_tok, (((0,), (0,)), ((), ())),
        precision=lax.Precision.HIGHEST, preferred_element_type=jnp.float32,
    )
    pieces = jnp.concatenate([gram, OFF_SCALE * cross], axis=1)
    pieces = pieces.reshape(group, ROW_DEV, span_width + col_group)

    win_own = lax.dynamic_slice_in_dim(wins, lo_index * ROW_DEV, ROW_DEV, 1).astype(jnp.float32)
    diag = jnp.sum(win_own * win_own, axis=0)
    w_cols = lax.dynamic_slice_in_dim(w_local, tok_index * tok_cols, tok_cols, 0)
    diag_term = (1.0 - OFF_SCALE) * diag[:, None] * w_cols[:, :ROW_DEV].astype(jnp.float32).T
    is_self = (jnp.arange(group) == lo_index)[:, None, None]
    diag_part = jnp.where(is_self, diag_term[None], 0.0)

    send = jnp.concatenate([pieces, diag_part], axis=2)
    send = jnp.concatenate([send] * mp_count, axis=0)
    got = lax.all_to_all(send, ("mp", "lo"), 0, 0, tiled=True)
    got = jnp.sum(got.reshape(mp_count, group, ROW_DEV, -1), axis=0)

    gram = got[:, :, :span_width]
    slot = lax.broadcasted_iota(jnp.int32, gram.shape, 0)
    row_ids = lax.broadcasted_iota(jnp.int32, gram.shape, 1)
    col_ids = lax.broadcasted_iota(jnp.int32, gram.shape, 2)
    on_diag = (tok_index == hi_index) & (slot == lo_index) & (col_ids == row_ids)
    reduced = jnp.where(on_diag, gram, OFF_SCALE * gram)
    denominator = jnp.transpose(reduced, (1, 0, 2)).reshape(ROW_DEV, group * span_width)
    numerator = jnp.transpose(got[:, :, span_width:span_width + col_group], (1, 0, 2)).reshape(ROW_DEV, tok_cols)
    numerator = numerator + jnp.sum(got[:, :, span_width + col_group:], axis=0)
    return (denominator, numerator)


def solution(mesh):
    mp_count, blk_count, tok_count = (mesh.shape[a] for a in ("mp", "blk", "tok"))
    group = blk_count // tok_count
    devices = np.asarray(mesh.devices).reshape(mp_count, tok_count, group, tok_count)
    split = Mesh(devices, ("mp", "hi", "lo", "tok"))
    placed = (P("mp", "tok", ("hi", "lo")), P("mp", None, ("hi", "lo")))
    return jax.shard_map(
        local,
        mesh=split,
        in_specs=placed,
        out_specs=(P(("hi", "lo"), "tok"), P(("hi", "lo"), "tok")),
        check_vma=False,
    )
```

```python
import jax
import jax.numpy as jnp
import numpy as np
from jax import lax
from jax.sharding import Mesh, PartitionSpec as P

ROW_DEV = 32


OFF_SCALE = 0.9


def local(inputs, down_weight):
    x_local = inputs[0]
    w_local = down_weight[0]
    tokens, span_width = x_local.shape
    cols = w_local.shape[0]
    hi_index = lax.axis_index("hi")
    lo_index = lax.axis_index("lo")
    tok_index = lax.axis_index("tok")
    group = lax.axis_size("lo")
    hi_count = lax.axis_size("hi")
    tok_count = lax.axis_size("tok")
    mp_count = lax.axis_size("mp")
    blk_count = hi_count * group
    col_group = cols // blk_count
    tok_cols = cols // tok_count

    win_lo = lax.all_gather(x_local[:, :ROW_DEV], "lo", axis=1, tiled=True)
    wins = lax.all_gather(win_lo, "tok", axis=0, tiled=True)

    swap = [(h * tok_count + t, t * tok_count + h) for h in range(hi_count) for t in range(tok_count)]

    y_part = lax.dot_general(
        x_local, w_local, (((1,), (1,)), ((), ())), preferred_element_type=jnp.float32
    )
    y_parts = lax.all_to_all(y_part, ("hi", "lo"), 1, 0, tiled=True)
    y_mine = jnp.sum(y_parts.reshape(blk_count, tokens, col_group), axis=0)
    y_round = lax.reduce_precision(y_mine, exponent_bits=8, mantissa_bits=7)
    y_high = y_round.astype(jnp.bfloat16)
    y_low = (y_mine - y_round).astype(jnp.bfloat16)
    payload = jnp.concatenate([x_local, y_high, y_low], axis=1)
    payload = lax.ppermute(payload, ("hi", "tok"), swap)
    spread = jnp.broadcast_to(payload[None], (hi_count,) + payload.shape)
    full = lax.all_to_all(spread, "hi", 0, 0, tiled=True).reshape(hi_count * tokens, -1)
    x_full = full[:, :span_width]
    y_tok = full[:, span_width:span_width + col_group].astype(jnp.float32) + full[:, span_width + col_group:].astype(jnp.float32)

    gram = lax.dot_general(
        wins, x_full, (((0,), (0,)), ((), ())), preferred_element_type=jnp.float32
    )
    cross = lax.dot_general(
        wins.astype(jnp.float32), y_tok, (((0,), (0,)), ((), ())),
        precision=lax.Precision.HIGHEST, preferred_element_type=jnp.float32,
    )
    pieces = jnp.concatenate([gram, OFF_SCALE * cross], axis=1)
    pieces = pieces.reshape(group, ROW_DEV, span_width + col_group)

    win_own = lax.dynamic_slice_in_dim(wins, lo_index * ROW_DEV, ROW_DEV, 1).astype(jnp.float32)
    diag = jnp.sum(win_own * win_own, axis=0)
    w_cols = lax.dynamic_slice_in_dim(w_local, tok_index * tok_cols, tok_cols, 0)
    diag_term = (1.0 - OFF_SCALE) * diag[:, None] * w_cols[:, :ROW_DEV].astype(jnp.float32).T
    is_self = (jnp.arange(group) == lo_index)[:, None, None]
    diag_part = jnp.where(is_self, diag_term[None], 0.0)

    send = jnp.concatenate([pieces, diag_part], axis=2)
    send = jnp.concatenate([send] * mp_count, axis=0)
    got = lax.all_to_all(send, ("mp", "lo"), 0, 0, tiled=True)
    got = jnp.sum(got.reshape(mp_count, group, ROW_DEV, -1), axis=0)

    gram = got[:, :, :span_width]
    slot = lax.broadcasted_iota(jnp.int32, gram.shape, 0)
    row_ids = lax.broadcasted_iota(jnp.int32, gram.shape, 1)
    col_ids = lax.broadcasted_iota(jnp.int32, gram.shape, 2)
    on_diag = (tok_index == hi_index) & (slot == lo_index) & (col_ids == row_ids)
    reduced = jnp.where(on_diag, gram, OFF_SCALE * gram)
    denominator = jnp.transpose(reduced, (1, 0, 2)).reshape(ROW_DEV, group * span_width)
    numerator = jnp.transpose(got[:, :, span_width:span_width + col_group], (1, 0, 2)).reshape(ROW_DEV, tok_cols)
    numerator = numerator + jnp.sum(got[:, :, span_width + col_group:], axis=0)
    return (denominator, numerator)


def solution(mesh):
    mp_count, blk_count, tok_count = (mesh.shape[a] for a in ("mp", "blk", "tok"))
    group = blk_count // tok_count
    devices = np.asarray(mesh.devices).reshape(mp_count, tok_count, group, tok_count)
    split = Mesh(devices, ("mp", "hi", "lo", "tok"))
    placed = (P("mp", "tok", ("hi", "lo")), P("mp", None, ("hi", "lo")))
    return jax.shard_map(
        local,
        mesh=split,
        in_specs=placed,
        out_specs=(P(("hi", "lo"), "tok"), P(("hi", "lo"), "tok")),
        check_vma=False,
    )
```

```python
import jax
import jax.numpy as jnp
import numpy as np
from jax import lax
from jax.sharding import Mesh, PartitionSpec as P

ROW_DEV = 32


OFF_SCALE = 0.9


def local(inputs, down_weight):
    x_local = inputs[0]
    w_local = down_weight[0]
    tokens, span_width = x_local.shape
    cols = w_local.shape[0]
    hi_index = lax.axis_index("hi")
    lo_index = lax.axis_index("lo")
    tok_index = lax.axis_index("tok")
    group = lax.axis_size("lo")
    hi_count = lax.axis_size("hi")
    tok_count = lax.axis_size("tok")
    mp_count = lax.axis_size("mp")
    blk_count = hi_count * group
    col_group = cols // blk_count
    tok_cols = cols // tok_count

    swap = [(h * tok_count + t, t * tok_count + h) for h in range(hi_count) for t in range(tok_count)]

    y_part = lax.dot_general(
        x_local, w_local, (((1,), (1,)), ((), ())), preferred_element_type=jnp.float32
    )
    y_part_round = lax.reduce_precision(y_part, exponent_bits=8, mantissa_bits=7)
    y_part_high = y_part_round.astype(jnp.bfloat16).reshape(tokens, blk_count, col_group)
    y_part_low = (y_part - y_part_round).astype(jnp.bfloat16).reshape(tokens, blk_count, col_group)
    win_spread = jnp.broadcast_to(x_local[:, None, :ROW_DEV], (tokens, blk_count, ROW_DEV))
    send_y = jnp.concatenate([y_part_high, y_part_low, win_spread], axis=2)
    got_y = lax.all_to_all(send_y, ("hi", "lo"), 1, 1, tiled=True)
    y_mine = jnp.sum(
        got_y[:, :, :col_group].astype(jnp.float32) + got_y[:, :, col_group:2 * col_group].astype(jnp.float32),
        axis=1,
    )
    win_lo = lax.dynamic_slice_in_dim(got_y[:, :, 2 * col_group:], hi_index * group, group, 1)
    wins = lax.all_gather(win_lo.reshape(tokens, group * ROW_DEV), "tok", axis=0, tiled=True)
    y_round = lax.reduce_precision(y_mine, exponent_bits=8, mantissa_bits=7)
    y_high = y_round.astype(jnp.bfloat16)
    y_low = (y_mine - y_round).astype(jnp.bfloat16)
    payload = jnp.concatenate([x_local, y_high, y_low], axis=1)
    payload = lax.ppermute(payload, ("hi", "tok"), swap)
    spread = jnp.broadcast_to(payload[None], (hi_count,) + payload.shape)
    full = lax.all_to_all(spread, "hi", 0, 0, tiled=True).reshape(hi_count * tokens, -1)
    x_full = full[:, :span_width]
    y_tok = full[:, span_width:span_width + col_group].astype(jnp.float32) + full[:, span_width + col_group:].astype(jnp.float32)

    gram = lax.dot_general(
        wins, x_full, (((0,), (0,)), ((), ())), preferred_element_type=jnp.float32
    )
    cross = lax.dot_general(
        wins.astype(jnp.float32), y_tok, (((0,), (0,)), ((), ())),
        precision=lax.Precision.HIGHEST, preferred_element_type=jnp.float32,
    )
    pieces = jnp.concatenate([gram, OFF_SCALE * cross], axis=1)
    pieces = pieces.reshape(group, ROW_DEV, span_width + col_group)

    win_own = lax.dynamic_slice_in_dim(wins, lo_index * ROW_DEV, ROW_DEV, 1).astype(jnp.float32)
    diag = jnp.sum(win_own * win_own, axis=0)
    w_cols = lax.dynamic_slice_in_dim(w_local, tok_index * tok_cols, tok_cols, 0)
    diag_term = (1.0 - OFF_SCALE) * diag[:, None] * w_cols[:, :ROW_DEV].astype(jnp.float32).T
    is_self = (jnp.arange(group) == lo_index)[:, None, None]
    diag_part = jnp.where(is_self, diag_term[None], 0.0)

    send = jnp.concatenate([pieces, diag_part], axis=2)
    send = jnp.concatenate([send] * mp_count, axis=0)
    got = lax.all_to_all(send, ("mp", "lo"), 0, 0, tiled=True)
    got = jnp.sum(got.reshape(mp_count, group, ROW_DEV, -1), axis=0)

    gram = got[:, :, :span_width]
    slot = lax.broadcasted_iota(jnp.int32, gram.shape, 0)
    row_ids = lax.broadcasted_iota(jnp.int32, gram.shape, 1)
    col_ids = lax.broadcasted_iota(jnp.int32, gram.shape, 2)
    on_diag = (tok_index == hi_index) & (slot == lo_index) & (col_ids == row_ids)
    reduced = jnp.where(on_diag, gram, OFF_SCALE * gram)
    denominator = jnp.transpose(reduced, (1, 0, 2)).reshape(ROW_DEV, group * span_width)
    numerator = jnp.transpose(got[:, :, span_width:span_width + col_group], (1, 0, 2)).reshape(ROW_DEV, tok_cols)
    numerator = numerator + jnp.sum(got[:, :, span_width + col_group:], axis=0)
    return (denominator, numerator)


def solution(mesh):
    mp_count, blk_count, tok_count = (mesh.shape[a] for a in ("mp", "blk", "tok"))
    group = blk_count // tok_count
    devices = np.asarray(mesh.devices).reshape(mp_count, tok_count, group, tok_count)
    split = Mesh(devices, ("mp", "hi", "lo", "tok"))
    placed = (P("mp", "tok", ("hi", "lo")), P("mp", None, ("hi", "lo")))
    return jax.shard_map(
        local,
        mesh=split,
        in_specs=placed,
        out_specs=(P(("hi", "lo"), "tok"), P(("hi", "lo"), "tok")),
        check_vma=False,
    )
```

```python
import jax
import jax.numpy as jnp
import numpy as np
from jax import lax
from jax.experimental import pallas as pl
from jax.experimental.pallas import tpu as pltpu
from jax.sharding import Mesh, PartitionSpec as P

ROW_DEV = 32


OFF_SCALE = 0.9


def _send_kernel(copies, group, span_width, wt_ref, full_ref, y_ref, tail_ref, out_ref):
    wt = wt_ref[...]
    gram = jnp.dot(wt, full_ref[:, :span_width], preferred_element_type=jnp.float32)
    cross = jnp.dot(
        wt.astype(jnp.float32), y_ref[...],
        precision=lax.Precision.HIGHEST, preferred_element_type=jnp.float32,
    )
    tail = OFF_SCALE * cross + tail_ref[...]
    for m in range(copies):
        for s in range(group):
            out_ref[m * group + s, :, :span_width] = gram[s * ROW_DEV:(s + 1) * ROW_DEV]
            out_ref[m * group + s, :, span_width:] = tail[s * ROW_DEV:(s + 1) * ROW_DEV]


def send_buffer(wins_t, full, y_wide, tail, copies, group, span_width):
    width = span_width + tail.shape[1]
    return pl.pallas_call(
        lambda *refs: _send_kernel(copies, group, span_width, *refs),
        out_shape=jax.ShapeDtypeStruct((copies * group, ROW_DEV, width), jnp.float32),
        in_specs=[pl.BlockSpec(memory_space=pltpu.VMEM)] * 4,
        out_specs=pl.BlockSpec(memory_space=pltpu.VMEM),
    )(wins_t, full, y_wide, tail)


def local(inputs, down_weight):
    x_local = inputs[0]
    w_local = down_weight[0]
    tokens, span_width = x_local.shape
    cols = w_local.shape[0]
    hi_index = lax.axis_index("hi")
    lo_index = lax.axis_index("lo")
    tok_index = lax.axis_index("tok")
    group = lax.axis_size("lo")
    hi_count = lax.axis_size("hi")
    tok_count = lax.axis_size("tok")
    mp_count = lax.axis_size("mp")
    blk_count = hi_count * group
    col_group = cols // blk_count
    tok_cols = cols // tok_count

    swap = [(h * tok_count + t, t * tok_count + h) for h in range(hi_count) for t in range(tok_count)]

    y_part = lax.dot_general(
        x_local, w_local, (((1,), (1,)), ((), ())), preferred_element_type=jnp.float32
    )
    y_part_round = lax.reduce_precision(y_part, exponent_bits=8, mantissa_bits=7)
    y_part_high = y_part_round.astype(jnp.bfloat16).reshape(tokens, blk_count, col_group)
    y_part_low = (y_part - y_part_round).astype(jnp.bfloat16).reshape(tokens, blk_count, col_group)
    win_spread = jnp.broadcast_to(x_local[:, None, :ROW_DEV], (tokens, blk_count, ROW_DEV))
    send_y = jnp.concatenate([y_part_high, y_part_low, win_spread], axis=2)
    got_y = lax.all_to_all(send_y, ("hi", "lo"), 1, 1, tiled=True)
    y_mine = jnp.sum(
        got_y[:, :, :col_group].astype(jnp.float32) + got_y[:, :, col_group:2 * col_group].astype(jnp.float32),
        axis=1,
    )
    win_lo = lax.dynamic_slice_in_dim(got_y[:, :, 2 * col_group:], hi_index * group, group, 1)
    wins = lax.all_gather(win_lo.reshape(tokens, group * ROW_DEV), "tok", axis=0, tiled=True)
    y_round = lax.reduce_precision(y_mine, exponent_bits=8, mantissa_bits=7)
    y_high = y_round.astype(jnp.bfloat16)
    y_low = (y_mine - y_round).astype(jnp.bfloat16)
    payload = jnp.concatenate([x_local, y_high, y_low], axis=1)
    payload = lax.ppermute(payload, ("hi", "tok"), swap)
    spread = jnp.broadcast_to(payload[None], (hi_count,) + payload.shape)
    full = lax.all_to_all(spread, "hi", 0, 0, tiled=True).reshape(hi_count * tokens, -1)
    y_tok = full[:, span_width:span_width + col_group].astype(jnp.float32) + full[:, span_width + col_group:].astype(jnp.float32)

    win_own = lax.dynamic_slice_in_dim(wins, lo_index * ROW_DEV, ROW_DEV, 1).astype(jnp.float32)
    diag = jnp.sum(win_own * win_own, axis=0)
    w_cols = lax.dynamic_slice_in_dim(w_local, tok_index * tok_cols, tok_cols, 0)
    diag_term = (1.0 - OFF_SCALE) * diag[:, None] * w_cols[:, :ROW_DEV].astype(jnp.float32).T
    is_self = (jnp.arange(group) == lo_index)[:, None, None]
    diag_part = jnp.where(is_self, diag_term[None], 0.0).reshape(group * ROW_DEV, tok_cols)

    y_wide = jnp.pad(y_tok, ((0, 0), (0, tok_cols)))
    tail = jnp.pad(diag_part, ((0, 0), (col_group, 0)))
    send = send_buffer(wins.T, full, y_wide, tail, mp_count, group, span_width)
    got = lax.all_to_all(send, ("mp", "lo"), 0, 0, tiled=True)
    got = jnp.sum(got.reshape(mp_count, group, ROW_DEV, -1), axis=0)

    gram = got[:, :, :span_width]
    slot = lax.broadcasted_iota(jnp.int32, gram.shape, 0)
    row_ids = lax.broadcasted_iota(jnp.int32, gram.shape, 1)
    col_ids = lax.broadcasted_iota(jnp.int32, gram.shape, 2)
    on_diag = (tok_index == hi_index) & (slot == lo_index) & (col_ids == row_ids)
    reduced = jnp.where(on_diag, gram, OFF_SCALE * gram)
    denominator = jnp.transpose(reduced, (1, 0, 2)).reshape(ROW_DEV, group * span_width)
    numerator = jnp.transpose(got[:, :, span_width:span_width + col_group], (1, 0, 2)).reshape(ROW_DEV, tok_cols)
    numerator = numerator + jnp.sum(got[:, :, span_width + col_group:], axis=0)
    return (denominator, numerator)


def solution(mesh):
    mp_count, blk_count, tok_count = (mesh.shape[a] for a in ("mp", "blk", "tok"))
    group = blk_count // tok_count
    devices = np.asarray(mesh.devices).reshape(mp_count, tok_count, group, tok_count)
    split = Mesh(devices, ("mp", "hi", "lo", "tok"))
    placed = (P("mp", "tok", ("hi", "lo")), P("mp", None, ("hi", "lo")))
    return jax.shard_map(
        local,
        mesh=split,
        in_specs=placed,
        out_specs=(P(("hi", "lo"), "tok"), P(("hi", "lo"), "tok")),
        check_vma=False,
    )
```

```python
import jax
import jax.numpy as jnp
import numpy as np
from jax import lax
from jax.sharding import Mesh, PartitionSpec as P

ROW_DEV = 32


OFF_SCALE = 0.9


def local(inputs, down_weight):
    x_local = inputs[0]
    w_local = down_weight[0]
    tokens, span_width = x_local.shape
    cols = w_local.shape[0]
    hi_index = lax.axis_index("hi")
    lo_index = lax.axis_index("lo")
    tok_index = lax.axis_index("tok")
    group = lax.axis_size("lo")
    hi_count = lax.axis_size("hi")
    tok_count = lax.axis_size("tok")
    mp_count = lax.axis_size("mp")
    blk_count = hi_count * group
    col_group = cols // blk_count
    tok_cols = cols // tok_count

    swap = [(h * tok_count + t, t * tok_count + h) for h in range(hi_count) for t in range(tok_count)]

    y_part = lax.dot_general(
        x_local, w_local, (((1,), (1,)), ((), ())), preferred_element_type=jnp.float32
    )
    y_part_round = lax.reduce_precision(y_part, exponent_bits=8, mantissa_bits=7)
    y_part_high = y_part_round.astype(jnp.bfloat16).reshape(tokens, blk_count, col_group)
    y_part_low = (y_part - y_part_round).astype(jnp.bfloat16).reshape(tokens, blk_count, col_group)
    win_spread = jnp.broadcast_to(x_local[:, None, :ROW_DEV], (tokens, blk_count, ROW_DEV))
    send_y = jnp.concatenate([y_part_high, y_part_low, win_spread], axis=2)
    got_y = lax.all_to_all(send_y, ("hi", "lo"), 1, 1, tiled=True)
    y_mine = jnp.sum(
        got_y[:, :, :col_group].astype(jnp.float32) + got_y[:, :, col_group:2 * col_group].astype(jnp.float32),
        axis=1,
    )
    win_lo = lax.dynamic_slice_in_dim(got_y[:, :, 2 * col_group:], hi_index * group, group, 1)
    win_lo = win_lo.reshape(tokens, group * ROW_DEV)
    win_spread = jnp.broadcast_to(win_lo[None], (tok_count,) + win_lo.shape)
    wins = lax.all_to_all(win_spread, "tok", 0, 0, tiled=True).reshape(tok_count * tokens, group * ROW_DEV)
    y_round = lax.reduce_precision(y_mine, exponent_bits=8, mantissa_bits=7)
    y_high = y_round.astype(jnp.bfloat16)
    y_low = (y_mine - y_round).astype(jnp.bfloat16)
    payload = jnp.concatenate([x_local, y_high, y_low], axis=1)
    payload = lax.ppermute(payload, ("hi", "tok"), swap)
    spread = jnp.broadcast_to(payload[None], (hi_count,) + payload.shape)
    full = lax.all_to_all(spread, "hi", 0, 0, tiled=True).reshape(hi_count * tokens, -1)
    x_full = full[:, :span_width]
    y_tok = full[:, span_width:span_width + col_group].astype(jnp.float32) + full[:, span_width + col_group:].astype(jnp.float32)

    gram = lax.dot_general(
        wins, x_full, (((0,), (0,)), ((), ())), preferred_element_type=jnp.float32
    )
    cross = lax.dot_general(
        wins.astype(jnp.float32), y_tok, (((0,), (0,)), ((), ())),
        precision=lax.Precision.HIGHEST, preferred_element_type=jnp.float32,
    )
    pieces = jnp.concatenate([gram, OFF_SCALE * cross], axis=1)
    pieces = pieces.reshape(group, ROW_DEV, span_width + col_group)

    win_own = lax.dynamic_slice_in_dim(wins, lo_index * ROW_DEV, ROW_DEV, 1).astype(jnp.float32)
    diag = jnp.sum(win_own * win_own, axis=0)
    w_cols = lax.dynamic_slice_in_dim(w_local, tok_index * tok_cols, tok_cols, 0)
    diag_term = (1.0 - OFF_SCALE) * diag[:, None] * w_cols[:, :ROW_DEV].astype(jnp.float32).T
    is_self = (jnp.arange(group) == lo_index)[:, None, None]
    diag_part = jnp.where(is_self, diag_term[None], 0.0)

    send = jnp.concatenate([pieces, diag_part], axis=2)
    send = jnp.concatenate([send] * mp_count, axis=0)
    got = lax.all_to_all(send, ("mp", "lo"), 0, 0, tiled=True)
    got = jnp.sum(got.reshape(mp_count, group, ROW_DEV, -1), axis=0)

    gram = got[:, :, :span_width]
    slot = lax.broadcasted_iota(jnp.int32, gram.shape, 0)
    row_ids = lax.broadcasted_iota(jnp.int32, gram.shape, 1)
    col_ids = lax.broadcasted_iota(jnp.int32, gram.shape, 2)
    on_diag = (tok_index == hi_index) & (slot == lo_index) & (col_ids == row_ids)
    reduced = jnp.where(on_diag, gram, OFF_SCALE * gram)
    denominator = jnp.transpose(reduced, (1, 0, 2)).reshape(ROW_DEV, group * span_width)
    numerator = jnp.transpose(got[:, :, span_width:span_width + col_group], (1, 0, 2)).reshape(ROW_DEV, tok_cols)
    numerator = numerator + jnp.sum(got[:, :, span_width + col_group:], axis=0)
    return (denominator, numerator)


def solution(mesh):
    mp_count, blk_count, tok_count = (mesh.shape[a] for a in ("mp", "blk", "tok"))
    group = blk_count // tok_count
    devices = np.asarray(mesh.devices).reshape(mp_count, tok_count, group, tok_count)
    split = Mesh(devices, ("mp", "hi", "lo", "tok"))
    placed = (P("mp", "tok", ("hi", "lo")), P("mp", None, ("hi", "lo")))
    return jax.shard_map(
        local,
        mesh=split,
        in_specs=placed,
        out_specs=(P(("hi", "lo"), "tok"), P(("hi", "lo"), "tok")),
        check_vma=False,
    )
```

```python
import jax
import jax.numpy as jnp
import numpy as np
from jax import lax
from jax.sharding import Mesh, PartitionSpec as P

ROW_DEV = 32


OFF_SCALE = 0.9


def local(inputs, down_weight):
    x_local = inputs[0]
    w_local = down_weight[0]
    tokens, span_width = x_local.shape
    cols = w_local.shape[0]
    hi_index = lax.axis_index("hi")
    lo_index = lax.axis_index("lo")
    tok_index = lax.axis_index("tok")
    group = lax.axis_size("lo")
    hi_count = lax.axis_size("hi")
    tok_count = lax.axis_size("tok")
    mp_count = lax.axis_size("mp")
    blk_count = hi_count * group
    col_group = cols // blk_count
    tok_cols = cols // tok_count

    swap = [(h * tok_count + t, t * tok_count + h) for h in range(hi_count) for t in range(tok_count)]

    y_part = lax.dot_general(
        x_local, w_local, (((1,), (1,)), ((), ())), preferred_element_type=jnp.float32
    )
    y_part_round = lax.reduce_precision(y_part, exponent_bits=8, mantissa_bits=7)
    y_part_high = y_part_round.astype(jnp.bfloat16).reshape(tokens, blk_count, col_group)
    y_part_low = (y_part - y_part_round).astype(jnp.bfloat16).reshape(tokens, blk_count, col_group)
    win_spread = jnp.broadcast_to(x_local[:, None, :ROW_DEV], (tokens, blk_count, ROW_DEV))
    send_y = jnp.concatenate([y_part_high, y_part_low, win_spread], axis=2)
    got_y = lax.all_to_all(send_y, ("hi", "lo"), 1, 1, tiled=True)
    y_mine = jnp.sum(
        got_y[:, :, :col_group].astype(jnp.float32) + got_y[:, :, col_group:2 * col_group].astype(jnp.float32),
        axis=1,
    )
    win_lo = lax.dynamic_slice_in_dim(got_y[:, :, 2 * col_group:], hi_index * group, group, 1)
    wins = lax.all_gather(win_lo.reshape(tokens, group * ROW_DEV), "tok", axis=0, tiled=True)
    y_round = lax.reduce_precision(y_mine, exponent_bits=8, mantissa_bits=7)
    y_high = y_round.astype(jnp.bfloat16)
    y_low = (y_mine - y_round).astype(jnp.bfloat16)
    payload = jnp.concatenate([x_local, y_high, y_low], axis=1)
    payload = lax.ppermute(payload, ("hi", "tok"), swap)
    spread = jnp.broadcast_to(payload[None], (hi_count,) + payload.shape)
    full = lax.all_to_all(spread, "hi", 0, 0, tiled=True).reshape(hi_count * tokens, -1)
    x_full = full[:, :span_width]
    y_tok = full[:, span_width:span_width + col_group].astype(jnp.float32) + full[:, span_width + col_group:].astype(jnp.float32)

    gram = lax.dot_general(
        wins, x_full, (((0,), (0,)), ((), ())), preferred_element_type=jnp.float32
    )
    cross = lax.dot_general(
        wins.astype(jnp.float32), y_tok, (((0,), (0,)), ((), ())),
        precision=lax.Precision.HIGHEST, preferred_element_type=jnp.float32,
    )
    pieces = jnp.concatenate([gram, OFF_SCALE * cross], axis=1)
    pieces = pieces.reshape(group, ROW_DEV, span_width + col_group)

    win_own = lax.dynamic_slice_in_dim(wins, lo_index * ROW_DEV, ROW_DEV, 1).astype(jnp.float32)
    diag = jnp.sum(win_own * win_own, axis=0)
    w_cols = lax.dynamic_slice_in_dim(w_local, tok_index * tok_cols, tok_cols, 0)
    diag_term = (1.0 - OFF_SCALE) * diag[:, None] * w_cols[:, :ROW_DEV].astype(jnp.float32).T
    is_self = (jnp.arange(group) == lo_index)[:, None, None]
    diag_part = jnp.where(is_self, diag_term[None], 0.0)

    send = jnp.concatenate([pieces, diag_part], axis=2)
    send = send + lax.ppermute(send, "mp", [(m, (m + 1) % mp_count) for m in range(mp_count)])
    got = lax.all_to_all(send, "lo", 0, 0, tiled=True)

    gram = got[:, :, :span_width]
    slot = lax.broadcasted_iota(jnp.int32, gram.shape, 0)
    row_ids = lax.broadcasted_iota(jnp.int32, gram.shape, 1)
    col_ids = lax.broadcasted_iota(jnp.int32, gram.shape, 2)
    on_diag = (tok_index == hi_index) & (slot == lo_index) & (col_ids == row_ids)
    reduced = jnp.where(on_diag, gram, OFF_SCALE * gram)
    denominator = jnp.transpose(reduced, (1, 0, 2)).reshape(ROW_DEV, group * span_width)
    numerator = jnp.transpose(got[:, :, span_width:span_width + col_group], (1, 0, 2)).reshape(ROW_DEV, tok_cols)
    numerator = numerator + jnp.sum(got[:, :, span_width + col_group:], axis=0)
    return (denominator, numerator)


def solution(mesh):
    mp_count, blk_count, tok_count = (mesh.shape[a] for a in ("mp", "blk", "tok"))
    group = blk_count // tok_count
    devices = np.asarray(mesh.devices).reshape(mp_count, tok_count, group, tok_count)
    split = Mesh(devices, ("mp", "hi", "lo", "tok"))
    placed = (P("mp", "tok", ("hi", "lo")), P("mp", None, ("hi", "lo")))
    return jax.shard_map(
        local,
        mesh=split,
        in_specs=placed,
        out_specs=(P(("hi", "lo"), "tok"), P(("hi", "lo"), "tok")),
        check_vma=False,
    )
```

```python
import jax
import jax.numpy as jnp
import numpy as np
from jax import lax
from jax.sharding import Mesh, PartitionSpec as P

ROW_DEV = 32
HI = ("hx", "hy")


OFF_SCALE = 0.9


def local(inputs, down_weight):
    x_local = inputs[0]
    w_local = down_weight[0]
    tokens, span_width = x_local.shape
    cols = w_local.shape[0]
    hi_index = lax.axis_index(HI)
    lo_index = lax.axis_index("lo")
    tok_index = lax.axis_index("tok")
    group = lax.axis_size("lo")
    hi_count = lax.axis_size(HI)
    half_count = lax.axis_size("hx")
    hy_index = lax.axis_index("hy")
    tok_count = lax.axis_size("tok")
    mp_count = lax.axis_size("mp")
    blk_count = hi_count * group
    col_group = cols // blk_count
    tok_cols = cols // tok_count

    swap = [(h * tok_count + t, t * tok_count + h) for h in range(hi_count) for t in range(tok_count)]

    y_part = lax.dot_general(
        x_local, w_local, (((1,), (1,)), ((), ())), preferred_element_type=jnp.float32
    )
    y_part_round = lax.reduce_precision(y_part, exponent_bits=8, mantissa_bits=7)
    y_part_high = y_part_round.astype(jnp.bfloat16).reshape(tokens, blk_count, col_group)
    y_part_low = (y_part - y_part_round).astype(jnp.bfloat16).reshape(tokens, blk_count, col_group)
    win_spread = jnp.broadcast_to(x_local[:, None, :ROW_DEV], (tokens, blk_count, ROW_DEV))
    send_y = jnp.concatenate([y_part_high, y_part_low, win_spread], axis=2)
    got_y = lax.all_to_all(send_y, HI + ("lo",), 1, 1, tiled=True)
    y_mine = jnp.sum(
        got_y[:, :, :col_group].astype(jnp.float32) + got_y[:, :, col_group:2 * col_group].astype(jnp.float32),
        axis=1,
    )
    win_lo = lax.dynamic_slice_in_dim(got_y[:, :, 2 * col_group:], hi_index * group, group, 1)
    wins = lax.all_gather(win_lo.reshape(tokens, group * ROW_DEV), "tok", axis=0, tiled=True)
    y_round = lax.reduce_precision(y_mine, exponent_bits=8, mantissa_bits=7)
    y_high = y_round.astype(jnp.bfloat16)
    y_low = (y_mine - y_round).astype(jnp.bfloat16)
    payload = jnp.concatenate([x_local, y_high, y_low], axis=1)
    mirror = [(h * tok_count + t, (t ^ 1) * tok_count + h) for h in range(hi_count) for t in range(tok_count)]
    own = lax.ppermute(payload, HI + ("tok",), swap)
    other = lax.ppermute(payload, HI + ("tok",), mirror)
    even_first = hy_index == 0
    pair = jnp.stack([jnp.where(even_first, own, other), jnp.where(even_first, other, own)])
    spread = jnp.broadcast_to(pair[None], (half_count,) + pair.shape)
    full = lax.all_to_all(spread, "hx", 0, 0, tiled=True).reshape(hi_count * tokens, -1)
    x_full = full[:, :span_width]
    y_tok = full[:, span_width:span_width + col_group].astype(jnp.float32) + full[:, span_width + col_group:].astype(jnp.float32)

    gram = lax.dot_general(
        wins, x_full, (((0,), (0,)), ((), ())), preferred_element_type=jnp.float32
    )
    cross = lax.dot_general(
        wins.astype(jnp.float32), y_tok, (((0,), (0,)), ((), ())),
        precision=lax.Precision.HIGHEST, preferred_element_type=jnp.float32,
    )
    pieces = jnp.concatenate([gram, OFF_SCALE * cross], axis=1)
    pieces = pieces.reshape(group, ROW_DEV, span_width + col_group)

    win_own = lax.dynamic_slice_in_dim(wins, lo_index * ROW_DEV, ROW_DEV, 1).astype(jnp.float32)
    diag = jnp.sum(win_own * win_own, axis=0)
    w_cols = lax.dynamic_slice_in_dim(w_local, tok_index * tok_cols, tok_cols, 0)
    diag_term = (1.0 - OFF_SCALE) * diag[:, None] * w_cols[:, :ROW_DEV].astype(jnp.float32).T
    is_self = (jnp.arange(group) == lo_index)[:, None, None]
    diag_part = jnp.where(is_self, diag_term[None], 0.0)

    send = jnp.concatenate([pieces, diag_part], axis=2)
    send = jnp.concatenate([send] * mp_count, axis=0)
    got = lax.all_to_all(send, ("mp", "lo"), 0, 0, tiled=True)
    got = jnp.sum(got.reshape(mp_count, group, ROW_DEV, -1), axis=0)

    gram = got[:, :, :span_width]
    slot = lax.broadcasted_iota(jnp.int32, gram.shape, 0)
    row_ids = lax.broadcasted_iota(jnp.int32, gram.shape, 1)
    col_ids = lax.broadcasted_iota(jnp.int32, gram.shape, 2)
    on_diag = (tok_index == hi_index) & (slot == lo_index) & (col_ids == row_ids)
    reduced = jnp.where(on_diag, gram, OFF_SCALE * gram)
    denominator = jnp.transpose(reduced, (1, 0, 2)).reshape(ROW_DEV, group * span_width)
    numerator = jnp.transpose(got[:, :, span_width:span_width + col_group], (1, 0, 2)).reshape(ROW_DEV, tok_cols)
    numerator = numerator + jnp.sum(got[:, :, span_width + col_group:], axis=0)
    return (denominator, numerator)


def solution(mesh):
    mp_count, blk_count, tok_count = (mesh.shape[a] for a in ("mp", "blk", "tok"))
    group = blk_count // tok_count
    devices = np.asarray(mesh.devices).reshape(mp_count, tok_count // 2, 2, group, tok_count)
    split = Mesh(devices, ("mp",) + HI + ("lo", "tok"))
    placed = (P("mp", "tok", HI + ("lo",)), P("mp", None, HI + ("lo",)))
    return jax.shard_map(
        local,
        mesh=split,
        in_specs=placed,
        out_specs=(P(HI + ("lo",), "tok"), P(HI + ("lo",), "tok")),
        check_vma=False,
    )
```

```python
import jax
import jax.numpy as jnp
import numpy as np
from jax import lax
from jax.sharding import Mesh, PartitionSpec as P

ROW_DEV = 32
HI = ("hx", "hy")


OFF_SCALE = 0.9


def local(inputs, down_weight):
    x_local = inputs[0]
    w_local = down_weight[0]
    tokens, span_width = x_local.shape
    cols = w_local.shape[0]
    hi_index = lax.axis_index(HI)
    lo_index = lax.axis_index("lo")
    tok_index = lax.axis_index("tok")
    group = lax.axis_size("lo")
    hi_count = lax.axis_size(HI)
    half_count = lax.axis_size("hx")
    hy_index = lax.axis_index("hy")
    tok_count = lax.axis_size("tok")
    mp_count = lax.axis_size("mp")
    blk_count = hi_count * group
    col_group = cols // blk_count
    tok_cols = cols // tok_count

    swap = [(h * tok_count + t, t * tok_count + h) for h in range(hi_count) for t in range(tok_count)]

    y_part = lax.dot_general(
        x_local, w_local, (((1,), (1,)), ((), ())), preferred_element_type=jnp.float32
    )
    y_part_round = lax.reduce_precision(y_part, exponent_bits=8, mantissa_bits=7)
    y_part_high = y_part_round.astype(jnp.bfloat16).reshape(tokens, blk_count, col_group)
    y_part_low = (y_part - y_part_round).astype(jnp.bfloat16).reshape(tokens, blk_count, col_group)
    win_spread = jnp.broadcast_to(x_local[:, None, :ROW_DEV], (tokens, blk_count, ROW_DEV))
    send_y = jnp.concatenate([y_part_high, y_part_low, win_spread], axis=2)
    got_y = lax.all_to_all(send_y, HI + ("lo",), 1, 1, tiled=True)
    y_mine = jnp.sum(
        got_y[:, :, :col_group].astype(jnp.float32) + got_y[:, :, col_group:2 * col_group].astype(jnp.float32),
        axis=1,
    )
    win_lo = lax.dynamic_slice_in_dim(got_y[:, :, 2 * col_group:], hi_index * group, group, 1)
    wins = lax.all_gather(win_lo.reshape(tokens, group * ROW_DEV), "tok", axis=0, tiled=True)
    y_round = lax.reduce_precision(y_mine, exponent_bits=8, mantissa_bits=7)
    y_high = y_round.astype(jnp.bfloat16)
    y_low = (y_mine - y_round).astype(jnp.bfloat16)
    payload = jnp.concatenate([x_local, y_high, y_low], axis=1)
    mirror = [(h * tok_count + t, (t ^ 1) * tok_count + h) for h in range(hi_count) for t in range(tok_count)]
    own = lax.ppermute(payload, HI + ("tok",), swap)
    other = lax.ppermute(payload, HI + ("tok",), mirror)
    even_first = hy_index == 0
    pair = jnp.stack([jnp.where(even_first, own, other), jnp.where(even_first, other, own)])
    spread = jnp.broadcast_to(pair[None], (half_count,) + pair.shape)
    full = lax.all_to_all(spread, "hx", 0, 0, tiled=True)
    x_full = full[..., :span_width]
    y_tok = full[..., span_width:span_width + col_group].astype(jnp.float32) + full[..., span_width + col_group:].astype(jnp.float32)

    wins_split = wins.reshape(full.shape[:3] + (wins.shape[1],))
    over_tokens = (((0, 1, 2), (0, 1, 2)), ((), ()))
    gram = lax.dot_general(wins_split, x_full, over_tokens, preferred_element_type=jnp.float32)
    cross = lax.dot_general(
        wins_split.astype(jnp.float32), y_tok, over_tokens,
        precision=lax.Precision.HIGHEST, preferred_element_type=jnp.float32,
    )
    pieces = jnp.concatenate([gram, OFF_SCALE * cross], axis=1)
    pieces = pieces.reshape(group, ROW_DEV, span_width + col_group)

    win_own = lax.dynamic_slice_in_dim(wins, lo_index * ROW_DEV, ROW_DEV, 1).astype(jnp.float32)
    diag = jnp.sum(win_own * win_own, axis=0)
    w_cols = lax.dynamic_slice_in_dim(w_local, tok_index * tok_cols, tok_cols, 0)
    diag_term = (1.0 - OFF_SCALE) * diag[:, None] * w_cols[:, :ROW_DEV].astype(jnp.float32).T
    is_self = (jnp.arange(group) == lo_index)[:, None, None]
    diag_part = jnp.where(is_self, diag_term[None], 0.0)

    send = jnp.concatenate([pieces, diag_part], axis=2)
    send = jnp.concatenate([send] * mp_count, axis=0)
    got = lax.all_to_all(send, ("mp", "lo"), 0, 0, tiled=True)
    got = jnp.sum(got.reshape(mp_count, group, ROW_DEV, -1), axis=0)

    gram = got[:, :, :span_width]
    slot = lax.broadcasted_iota(jnp.int32, gram.shape, 0)
    row_ids = lax.broadcasted_iota(jnp.int32, gram.shape, 1)
    col_ids = lax.broadcasted_iota(jnp.int32, gram.shape, 2)
    on_diag = (tok_index == hi_index) & (slot == lo_index) & (col_ids == row_ids)
    reduced = jnp.where(on_diag, gram, OFF_SCALE * gram)
    denominator = jnp.transpose(reduced, (1, 0, 2)).reshape(ROW_DEV, group * span_width)
    numerator = jnp.transpose(got[:, :, span_width:span_width + col_group], (1, 0, 2)).reshape(ROW_DEV, tok_cols)
    numerator = numerator + jnp.sum(got[:, :, span_width + col_group:], axis=0)
    return (denominator, numerator)


def solution(mesh):
    mp_count, blk_count, tok_count = (mesh.shape[a] for a in ("mp", "blk", "tok"))
    group = blk_count // tok_count
    devices = np.asarray(mesh.devices).reshape(mp_count, tok_count // 2, 2, group, tok_count)
    split = Mesh(devices, ("mp",) + HI + ("lo", "tok"))
    placed = (P("mp", "tok", HI + ("lo",)), P("mp", None, HI + ("lo",)))
    return jax.shard_map(
        local,
        mesh=split,
        in_specs=placed,
        out_specs=(P(HI + ("lo",), "tok"), P(HI + ("lo",), "tok")),
        check_vma=False,
    )
```

```python
import jax
import jax.numpy as jnp
import numpy as np
from jax import lax
from jax.sharding import Mesh, PartitionSpec as P

ROW_DEV = 32
HI = ("hx", "hy")


OFF_SCALE = 0.9


def local(inputs, down_weight):
    x_local = inputs[0]
    w_local = down_weight[0]
    tokens, span_width = x_local.shape
    cols = w_local.shape[0]
    hi_index = lax.axis_index(HI)
    lo_index = lax.axis_index("lo")
    tok_index = lax.axis_index("tok")
    group = lax.axis_size("lo")
    hi_count = lax.axis_size(HI)
    half_count = lax.axis_size("hx")
    hy_index = lax.axis_index("hy")
    tok_count = lax.axis_size("tok")
    mp_count = lax.axis_size("mp")
    blk_count = hi_count * group
    col_group = cols // blk_count
    tok_cols = cols // tok_count

    swap = [(h * tok_count + t, t * tok_count + h) for h in range(hi_count) for t in range(tok_count)]

    y_part = lax.dot_general(
        x_local, w_local, (((1,), (1,)), ((), ())), preferred_element_type=jnp.float32
    )
    y_part_round = lax.reduce_precision(y_part, exponent_bits=8, mantissa_bits=7)
    y_part_high = y_part_round.astype(jnp.bfloat16).reshape(tokens, blk_count, col_group)
    y_part_low = (y_part - y_part_round).astype(jnp.bfloat16).reshape(tokens, blk_count, col_group)
    win_spread = jnp.broadcast_to(x_local[:, None, :ROW_DEV], (tokens, blk_count, ROW_DEV))
    send_y = jnp.concatenate([y_part_high, y_part_low, win_spread], axis=2)
    got_y = lax.all_to_all(send_y, HI + ("lo",), 1, 1, tiled=True)
    y_mine = jnp.sum(
        got_y[:, :, :col_group].astype(jnp.float32) + got_y[:, :, col_group:2 * col_group].astype(jnp.float32),
        axis=1,
    )
    win_lo = lax.dynamic_slice_in_dim(got_y[:, :, 2 * col_group:], hi_index * group, group, 1)
    wins = lax.all_gather(win_lo.reshape(tokens, group * ROW_DEV), "tok", axis=0, tiled=True)
    y_round = lax.reduce_precision(y_mine, exponent_bits=8, mantissa_bits=7)
    y_high = y_round.astype(jnp.bfloat16)
    y_low = (y_mine - y_round).astype(jnp.bfloat16)
    payload = jnp.concatenate([x_local, y_high, y_low], axis=1)
    mirror = [(h * tok_count + t, (t ^ 1) * tok_count + h) for h in range(hi_count) for t in range(tok_count)]
    own = lax.ppermute(payload, HI + ("tok",), swap)
    other = lax.ppermute(payload, HI + ("tok",), mirror)
    own, other, wins = lax.optimization_barrier((own, other, wins))
    even_first = hy_index == 0
    pair = jnp.stack([jnp.where(even_first, own, other), jnp.where(even_first, other, own)])
    spread = jnp.broadcast_to(pair[None], (half_count,) + pair.shape)
    full = lax.all_to_all(spread, "hx", 0, 0, tiled=True)
    x_full = full[..., :span_width]
    y_tok = full[..., span_width:span_width + col_group].astype(jnp.float32) + full[..., span_width + col_group:].astype(jnp.float32)

    wins_split = wins.reshape(full.shape[:3] + (wins.shape[1],))
    over_tokens = (((0, 1, 2), (0, 1, 2)), ((), ()))
    gram = lax.dot_general(wins_split, x_full, over_tokens, preferred_element_type=jnp.float32)
    cross = lax.dot_general(
        wins_split.astype(jnp.float32), y_tok, over_tokens,
        precision=lax.Precision.HIGHEST, preferred_element_type=jnp.float32,
    )
    pieces = jnp.concatenate([gram, OFF_SCALE * cross], axis=1)
    pieces = pieces.reshape(group, ROW_DEV, span_width + col_group)

    win_own = lax.dynamic_slice_in_dim(wins, lo_index * ROW_DEV, ROW_DEV, 1).astype(jnp.float32)
    diag = jnp.sum(win_own * win_own, axis=0)
    w_cols = lax.dynamic_slice_in_dim(w_local, tok_index * tok_cols, tok_cols, 0)
    diag_term = (1.0 - OFF_SCALE) * diag[:, None] * w_cols[:, :ROW_DEV].astype(jnp.float32).T
    is_self = (jnp.arange(group) == lo_index)[:, None, None]
    diag_part = jnp.where(is_self, diag_term[None], 0.0)

    send = jnp.concatenate([pieces, diag_part], axis=2)
    send = jnp.concatenate([send] * mp_count, axis=0)
    got = lax.all_to_all(send, ("mp", "lo"), 0, 0, tiled=True)
    got = jnp.sum(got.reshape(mp_count, group, ROW_DEV, -1), axis=0)

    gram = got[:, :, :span_width]
    slot = lax.broadcasted_iota(jnp.int32, gram.shape, 0)
    row_ids = lax.broadcasted_iota(jnp.int32, gram.shape, 1)
    col_ids = lax.broadcasted_iota(jnp.int32, gram.shape, 2)
    on_diag = (tok_index == hi_index) & (slot == lo_index) & (col_ids == row_ids)
    reduced = jnp.where(on_diag, gram, OFF_SCALE * gram)
    denominator = jnp.transpose(reduced, (1, 0, 2)).reshape(ROW_DEV, group * span_width)
    numerator = jnp.transpose(got[:, :, span_width:span_width + col_group], (1, 0, 2)).reshape(ROW_DEV, tok_cols)
    numerator = numerator + jnp.sum(got[:, :, span_width + col_group:], axis=0)
    return (denominator, numerator)


def solution(mesh):
    mp_count, blk_count, tok_count = (mesh.shape[a] for a in ("mp", "blk", "tok"))
    group = blk_count // tok_count
    devices = np.asarray(mesh.devices).reshape(mp_count, tok_count // 2, 2, group, tok_count)
    split = Mesh(devices, ("mp",) + HI + ("lo", "tok"))
    placed = (P("mp", "tok", HI + ("lo",)), P("mp", None, HI + ("lo",)))
    return jax.shard_map(
        local,
        mesh=split,
        in_specs=placed,
        out_specs=(P(HI + ("lo",), "tok"), P(HI + ("lo",), "tok")),
        check_vma=False,
    )
```

```python
import jax
import jax.numpy as jnp
import numpy as np
from jax import lax
from jax.sharding import Mesh, PartitionSpec as P

ROW_DEV = 32
HI = ("hx", "hy")


OFF_SCALE = 0.9


def local(inputs, down_weight):
    x_local = inputs[0]
    w_local = down_weight[0]
    tokens, span_width = x_local.shape
    cols = w_local.shape[0]
    hi_index = lax.axis_index(HI)
    lo_index = lax.axis_index("lo")
    tok_index = lax.axis_index("tok")
    group = lax.axis_size("lo")
    hi_count = lax.axis_size(HI)
    half_count = lax.axis_size("hx")
    hy_index = lax.axis_index("hy")
    tok_count = lax.axis_size("tok")
    mp_count = lax.axis_size("mp")
    blk_count = hi_count * group
    col_group = cols // blk_count
    tok_cols = cols // tok_count

    swap = [(h * tok_count + t, t * tok_count + h) for h in range(hi_count) for t in range(tok_count)]

    y_part = lax.dot_general(
        x_local, w_local, (((1,), (1,)), ((), ())), preferred_element_type=jnp.float32
    )
    y_part_round = lax.reduce_precision(y_part, exponent_bits=8, mantissa_bits=7)
    y_part_high = y_part_round.astype(jnp.bfloat16).reshape(tokens, blk_count, col_group)
    y_part_low = (y_part - y_part_round).astype(jnp.bfloat16).reshape(tokens, blk_count, col_group)
    win_spread = jnp.broadcast_to(x_local[:, None, :ROW_DEV], (tokens, blk_count, ROW_DEV))
    send_y = jnp.concatenate([y_part_high, y_part_low, win_spread], axis=2)
    got_y = lax.all_to_all(send_y, HI + ("lo",), 1, 1, tiled=True)
    y_mine = jnp.sum(
        got_y[:, :, :col_group].astype(jnp.float32) + got_y[:, :, col_group:2 * col_group].astype(jnp.float32),
        axis=1,
    )
    win_lo = lax.dynamic_slice_in_dim(got_y[:, :, 2 * col_group:], hi_index * group, group, 1)
    wins = lax.all_gather(win_lo.reshape(tokens, group * ROW_DEV), "tok", axis=0, tiled=True)
    y_round = lax.reduce_precision(y_mine, exponent_bits=8, mantissa_bits=7)
    y_high = y_round.astype(jnp.bfloat16)
    y_low = (y_mine - y_round).astype(jnp.bfloat16)
    mirror = [(h * tok_count + t, (t ^ 1) * tok_count + h) for h in range(hi_count) for t in range(tok_count)]
    x_own = lax.ppermute(x_local, HI + ("tok",), swap)
    x_other = lax.ppermute(x_local, HI + ("tok",), mirror)
    y_pay = jnp.concatenate([y_high, y_low], axis=1)
    own = jnp.concatenate([x_own, lax.ppermute(y_pay, HI + ("tok",), swap)], axis=1)
    other = jnp.concatenate([x_other, lax.ppermute(y_pay, HI + ("tok",), mirror)], axis=1)
    even_first = hy_index == 0
    pair = jnp.stack([jnp.where(even_first, own, other), jnp.where(even_first, other, own)])
    spread = jnp.broadcast_to(pair[None], (half_count,) + pair.shape)
    full = lax.all_to_all(spread, "hx", 0, 0, tiled=True)
    x_full = full[..., :span_width]
    y_tok = full[..., span_width:span_width + col_group].astype(jnp.float32) + full[..., span_width + col_group:].astype(jnp.float32)

    wins_split = wins.reshape(full.shape[:3] + (wins.shape[1],))
    over_tokens = (((0, 1, 2), (0, 1, 2)), ((), ()))
    gram = lax.dot_general(wins_split, x_full, over_tokens, preferred_element_type=jnp.float32)
    cross = lax.dot_general(
        wins_split.astype(jnp.float32), y_tok, over_tokens,
        precision=lax.Precision.HIGHEST, preferred_element_type=jnp.float32,
    )
    pieces = jnp.concatenate([gram, OFF_SCALE * cross], axis=1)
    pieces = pieces.reshape(group, ROW_DEV, span_width + col_group)

    win_own = lax.dynamic_slice_in_dim(wins, lo_index * ROW_DEV, ROW_DEV, 1).astype(jnp.float32)
    diag = jnp.sum(win_own * win_own, axis=0)
    w_cols = lax.dynamic_slice_in_dim(w_local, tok_index * tok_cols, tok_cols, 0)
    diag_term = (1.0 - OFF_SCALE) * diag[:, None] * w_cols[:, :ROW_DEV].astype(jnp.float32).T
    is_self = (jnp.arange(group) == lo_index)[:, None, None]
    diag_part = jnp.where(is_self, diag_term[None], 0.0)

    send = jnp.concatenate([pieces, diag_part], axis=2)
    send = jnp.concatenate([send] * mp_count, axis=0)
    got = lax.all_to_all(send, ("mp", "lo"), 0, 0, tiled=True)
    got = jnp.sum(got.reshape(mp_count, group, ROW_DEV, -1), axis=0)

    gram = got[:, :, :span_width]
    slot = lax.broadcasted_iota(jnp.int32, gram.shape, 0)
    row_ids = lax.broadcasted_iota(jnp.int32, gram.shape, 1)
    col_ids = lax.broadcasted_iota(jnp.int32, gram.shape, 2)
    on_diag = (tok_index == hi_index) & (slot == lo_index) & (col_ids == row_ids)
    reduced = jnp.where(on_diag, gram, OFF_SCALE * gram)
    denominator = jnp.transpose(reduced, (1, 0, 2)).reshape(ROW_DEV, group * span_width)
    numerator = jnp.transpose(got[:, :, span_width:span_width + col_group], (1, 0, 2)).reshape(ROW_DEV, tok_cols)
    numerator = numerator + jnp.sum(got[:, :, span_width + col_group:], axis=0)
    return (denominator, numerator)


def solution(mesh):
    mp_count, blk_count, tok_count = (mesh.shape[a] for a in ("mp", "blk", "tok"))
    group = blk_count // tok_count
    devices = np.asarray(mesh.devices).reshape(mp_count, tok_count // 2, 2, group, tok_count)
    split = Mesh(devices, ("mp",) + HI + ("lo", "tok"))
    placed = (P("mp", "tok", HI + ("lo",)), P("mp", None, HI + ("lo",)))
    return jax.shard_map(
        local,
        mesh=split,
        in_specs=placed,
        out_specs=(P(HI + ("lo",), "tok"), P(HI + ("lo",), "tok")),
        check_vma=False,
    )
```

```python
import jax
import jax.numpy as jnp
import numpy as np
from jax import lax
from jax.sharding import Mesh, PartitionSpec as P

ROW_DEV = 32
HI = ("hx", "hy")


OFF_SCALE = 0.9


def local(inputs, down_weight):
    x_local = inputs[0]
    w_local = down_weight[0]
    tokens, span_width = x_local.shape
    cols = w_local.shape[0]
    hi_index = lax.axis_index(HI)
    lo_index = lax.axis_index("lo")
    tok_index = lax.axis_index("tok")
    group = lax.axis_size("lo")
    hi_count = lax.axis_size(HI)
    half_count = lax.axis_size("hx")
    hy_index = lax.axis_index("hy")
    tok_count = lax.axis_size("tok")
    mp_count = lax.axis_size("mp")
    blk_count = hi_count * group
    col_group = cols // blk_count
    tok_cols = cols // tok_count

    swap = [(h * tok_count + t, t * tok_count + h) for h in range(hi_count) for t in range(tok_count)]

    y_part = lax.dot_general(
        x_local, w_local, (((1,), (1,)), ((), ())), preferred_element_type=jnp.float32
    )
    y_part_round = lax.reduce_precision(y_part, exponent_bits=8, mantissa_bits=7)
    y_part_high = y_part_round.astype(jnp.bfloat16).reshape(tokens, blk_count, col_group)
    y_part_low = (y_part - y_part_round).astype(jnp.bfloat16).reshape(tokens, blk_count, col_group)
    win_spread = jnp.broadcast_to(x_local[:, None, :ROW_DEV], (tokens, blk_count, ROW_DEV))
    send_y = jnp.concatenate([y_part_high, y_part_low, win_spread], axis=2)
    got_y = lax.all_to_all(send_y, HI + ("lo",), 1, 1, tiled=True)
    y_mine = jnp.sum(
        got_y[:, :, :col_group].astype(jnp.float32) + got_y[:, :, col_group:2 * col_group].astype(jnp.float32),
        axis=1,
    )
    win_lo = lax.dynamic_slice_in_dim(got_y[:, :, 2 * col_group:], hi_index * group, group, 1)
    wins = lax.all_gather(win_lo.reshape(tokens, group * ROW_DEV), "tok", axis=0, tiled=True)
    y_round = lax.reduce_precision(y_mine, exponent_bits=8, mantissa_bits=7)
    y_high = y_round.astype(jnp.bfloat16)
    y_low = (y_mine - y_round).astype(jnp.bfloat16)
    mirror = [(h * tok_count + t, (t ^ 1) * tok_count + h) for h in range(hi_count) for t in range(tok_count)]
    x_own = lax.ppermute(x_local, HI + ("tok",), swap)
    x_other = lax.ppermute(x_local, HI + ("tok",), mirror)
    y_pay = jnp.concatenate([y_high, y_low], axis=1)
    own = jnp.concatenate([x_own, lax.ppermute(y_pay, HI + ("tok",), swap)], axis=1)
    other = jnp.concatenate([x_other, lax.ppermute(y_pay, HI + ("tok",), mirror)], axis=1)
    own, other, wins = lax.optimization_barrier((own, other, wins))
    even_first = hy_index == 0
    pair = jnp.stack([jnp.where(even_first, own, other), jnp.where(even_first, other, own)])
    spread = jnp.broadcast_to(pair[None], (half_count,) + pair.shape)
    full = lax.all_to_all(spread, "hx", 0, 0, tiled=True)
    x_full = full[..., :span_width]
    y_tok = full[..., span_width:span_width + col_group].astype(jnp.float32) + full[..., span_width + col_group:].astype(jnp.float32)

    wins_split = wins.reshape(full.shape[:3] + (wins.shape[1],))
    over_tokens = (((0, 1, 2), (0, 1, 2)), ((), ()))
    gram = lax.dot_general(wins_split, x_full, over_tokens, preferred_element_type=jnp.float32)
    cross = lax.dot_general(
        wins_split.astype(jnp.float32), y_tok, over_tokens,
        precision=lax.Precision.HIGHEST, preferred_element_type=jnp.float32,
    )
    pieces = jnp.concatenate([gram, OFF_SCALE * cross], axis=1)
    pieces = pieces.reshape(group, ROW_DEV, span_width + col_group)

    win_own = lax.dynamic_slice_in_dim(wins, lo_index * ROW_DEV, ROW_DEV, 1).astype(jnp.float32)
    diag = jnp.sum(win_own * win_own, axis=0)
    w_cols = lax.dynamic_slice_in_dim(w_local, tok_index * tok_cols, tok_cols, 0)
    diag_term = (1.0 - OFF_SCALE) * diag[:, None] * w_cols[:, :ROW_DEV].astype(jnp.float32).T
    is_self = (jnp.arange(group) == lo_index)[:, None, None]
    diag_part = jnp.where(is_self, diag_term[None], 0.0)

    send = jnp.concatenate([pieces, diag_part], axis=2)
    send = jnp.concatenate([send] * mp_count, axis=0)
    got = lax.all_to_all(send, ("mp", "lo"), 0, 0, tiled=True)
    got = jnp.sum(got.reshape(mp_count, group, ROW_DEV, -1), axis=0)

    gram = got[:, :, :span_width]
    slot = lax.broadcasted_iota(jnp.int32, gram.shape, 0)
    row_ids = lax.broadcasted_iota(jnp.int32, gram.shape, 1)
    col_ids = lax.broadcasted_iota(jnp.int32, gram.shape, 2)
    on_diag = (tok_index == hi_index) & (slot == lo_index) & (col_ids == row_ids)
    reduced = jnp.where(on_diag, gram, OFF_SCALE * gram)
    denominator = jnp.transpose(reduced, (1, 0, 2)).reshape(ROW_DEV, group * span_width)
    numerator = jnp.transpose(got[:, :, span_width:span_width + col_group], (1, 0, 2)).reshape(ROW_DEV, tok_cols)
    numerator = numerator + jnp.sum(got[:, :, span_width + col_group:], axis=0)
    return (denominator, numerator)


def solution(mesh):
    mp_count, blk_count, tok_count = (mesh.shape[a] for a in ("mp", "blk", "tok"))
    group = blk_count // tok_count
    devices = np.asarray(mesh.devices).reshape(mp_count, tok_count // 2, 2, group, tok_count)
    split = Mesh(devices, ("mp",) + HI + ("lo", "tok"))
    placed = (P("mp", "tok", HI + ("lo",)), P("mp", None, HI + ("lo",)))
    return jax.shard_map(
        local,
        mesh=split,
        in_specs=placed,
        out_specs=(P(HI + ("lo",), "tok"), P(HI + ("lo",), "tok")),
        check_vma=False,
    )
```

```python
import jax
import jax.numpy as jnp
import numpy as np
from jax import lax
from jax.sharding import Mesh, PartitionSpec as P

ROW_DEV = 32
HI = ("hx", "hy")


OFF_SCALE = 0.9


def local(inputs, down_weight):
    x_local = inputs[0]
    w_local = down_weight[0]
    tokens, span_width = x_local.shape
    cols = w_local.shape[0]
    hi_index = lax.axis_index(HI)
    lo_index = lax.axis_index("lo")
    tok_index = lax.axis_index("tok")
    group = lax.axis_size("lo")
    hi_count = lax.axis_size(HI)
    half_count = lax.axis_size("hx")
    hy_index = lax.axis_index("hy")
    tok_count = lax.axis_size("tok")
    mp_count = lax.axis_size("mp")
    blk_count = hi_count * group
    col_group = cols // blk_count
    tok_cols = cols // tok_count

    swap = [(h * tok_count + t, t * tok_count + h) for h in range(hi_count) for t in range(tok_count)]

    mirror = [(h * tok_count + t, (t ^ 1) * tok_count + h) for h in range(hi_count) for t in range(tok_count)]
    x_own = lax.ppermute(x_local, HI + ("tok",), swap)
    x_other = lax.ppermute(x_local, HI + ("tok",), mirror)

    win_lo = lax.all_gather(x_local[:, :ROW_DEV], "lo", axis=1, tiled=True)
    wins = lax.all_gather(win_lo, "tok", axis=0, tiled=True)

    y_part = lax.dot_general(
        x_local, w_local, (((1,), (1,)), ((), ())), preferred_element_type=jnp.float32
    )
    y_part_round = lax.reduce_precision(y_part, exponent_bits=8, mantissa_bits=7)
    y_part_high = y_part_round.astype(jnp.bfloat16).reshape(tokens, blk_count, col_group)
    y_part_low = (y_part - y_part_round).astype(jnp.bfloat16).reshape(tokens, blk_count, col_group)
    send_y = jnp.concatenate([y_part_high, y_part_low], axis=2)
    got_y = lax.all_to_all(send_y, HI + ("lo",), 1, 1, tiled=True)
    got_y, wins = lax.optimization_barrier((got_y, wins))
    y_mine = jnp.sum(
        got_y[:, :, :col_group].astype(jnp.float32) + got_y[:, :, col_group:].astype(jnp.float32),
        axis=1,
    )
    y_round = lax.reduce_precision(y_mine, exponent_bits=8, mantissa_bits=7)
    y_high = y_round.astype(jnp.bfloat16)
    y_low = (y_mine - y_round).astype(jnp.bfloat16)
    y_pay = jnp.concatenate([y_high, y_low], axis=1)
    own = jnp.concatenate([x_own, lax.ppermute(y_pay, HI + ("tok",), swap)], axis=1)
    other = jnp.concatenate([x_other, lax.ppermute(y_pay, HI + ("tok",), mirror)], axis=1)
    even_first = hy_index == 0
    pair = jnp.stack([jnp.where(even_first, own, other), jnp.where(even_first, other, own)])
    spread = jnp.broadcast_to(pair[None], (half_count,) + pair.shape)
    full = lax.all_to_all(spread, "hx", 0, 0, tiled=True)
    x_full = full[..., :span_width]
    y_tok = full[..., span_width:span_width + col_group].astype(jnp.float32) + full[..., span_width + col_group:].astype(jnp.float32)

    wins_split = wins.reshape(full.shape[:3] + (wins.shape[1],))
    over_tokens = (((0, 1, 2), (0, 1, 2)), ((), ()))
    gram = lax.dot_general(wins_split, x_full, over_tokens, preferred_element_type=jnp.float32)
    cross = lax.dot_general(
        wins_split.astype(jnp.float32), y_tok, over_tokens,
        precision=lax.Precision.HIGHEST, preferred_element_type=jnp.float32,
    )
    pieces = jnp.concatenate([gram, OFF_SCALE * cross], axis=1)
    pieces = pieces.reshape(group, ROW_DEV, span_width + col_group)

    win_own = lax.dynamic_slice_in_dim(wins, lo_index * ROW_DEV, ROW_DEV, 1).astype(jnp.float32)
    diag = jnp.sum(win_own * win_own, axis=0)
    w_cols = lax.dynamic_slice_in_dim(w_local, tok_index * tok_cols, tok_cols, 0)
    diag_term = (1.0 - OFF_SCALE) * diag[:, None] * w_cols[:, :ROW_DEV].astype(jnp.float32).T
    is_self = (jnp.arange(group) == lo_index)[:, None, None]
    diag_part = jnp.where(is_self, diag_term[None], 0.0)

    send = jnp.concatenate([pieces, diag_part], axis=2)
    send = jnp.concatenate([send] * mp_count, axis=0)
    got = lax.all_to_all(send, ("mp", "lo"), 0, 0, tiled=True)
    got = jnp.sum(got.reshape(mp_count, group, ROW_DEV, -1), axis=0)

    gram = got[:, :, :span_width]
    slot = lax.broadcasted_iota(jnp.int32, gram.shape, 0)
    row_ids = lax.broadcasted_iota(jnp.int32, gram.shape, 1)
    col_ids = lax.broadcasted_iota(jnp.int32, gram.shape, 2)
    on_diag = (tok_index == hi_index) & (slot == lo_index) & (col_ids == row_ids)
    reduced = jnp.where(on_diag, gram, OFF_SCALE * gram)
    denominator = jnp.transpose(reduced, (1, 0, 2)).reshape(ROW_DEV, group * span_width)
    numerator = jnp.transpose(got[:, :, span_width:span_width + col_group], (1, 0, 2)).reshape(ROW_DEV, tok_cols)
    numerator = numerator + jnp.sum(got[:, :, span_width + col_group:], axis=0)
    return (denominator, numerator)


def solution(mesh):
    mp_count, blk_count, tok_count = (mesh.shape[a] for a in ("mp", "blk", "tok"))
    group = blk_count // tok_count
    devices = np.asarray(mesh.devices).reshape(mp_count, tok_count // 2, 2, group, tok_count)
    split = Mesh(devices, ("mp",) + HI + ("lo", "tok"))
    placed = (P("mp", "tok", HI + ("lo",)), P("mp", None, HI + ("lo",)))
    return jax.shard_map(
        local,
        mesh=split,
        in_specs=placed,
        out_specs=(P(HI + ("lo",), "tok"), P(HI + ("lo",), "tok")),
        check_vma=False,
    )
```

```python
import jax
import jax.numpy as jnp
import numpy as np
from jax import lax
from jax.sharding import Mesh, PartitionSpec as P

ROW_DEV = 32
HI = ("hx", "hy")


OFF_SCALE = 0.9


def local(inputs, down_weight):
    x_local = inputs[0]
    w_local = down_weight[0]
    tokens, span_width = x_local.shape
    cols = w_local.shape[0]
    hi_index = lax.axis_index(HI)
    lo_index = lax.axis_index("lo")
    tok_index = lax.axis_index("tok")
    group = lax.axis_size("lo")
    hi_count = lax.axis_size(HI)
    half_count = lax.axis_size("hx")
    hy_index = lax.axis_index("hy")
    tok_count = lax.axis_size("tok")
    mp_count = lax.axis_size("mp")
    blk_count = hi_count * group
    col_group = cols // blk_count
    tok_cols = cols // tok_count

    swap = [(h * tok_count + t, t * tok_count + h) for h in range(hi_count) for t in range(tok_count)]

    y_part = lax.dot_general(
        x_local, w_local, (((1,), (1,)), ((), ())), preferred_element_type=jnp.float32
    )
    y_part = y_part.reshape(tokens, half_count, 2, group, col_group)
    y_near = jnp.take(y_part, hy_index, axis=2).reshape(tokens, half_count * group, col_group)
    y_far = jnp.take(y_part, 1 - hy_index, axis=2).reshape(tokens, half_count * group, col_group)

    def halves(v):
        r = lax.reduce_precision(v, exponent_bits=8, mantissa_bits=7)
        return [r.astype(jnp.bfloat16), (v - r).astype(jnp.bfloat16)]

    win_spread = jnp.broadcast_to(x_local[:, None, :ROW_DEV], (tokens, half_count * group, ROW_DEV))
    send_y = jnp.concatenate(halves(y_near) + halves(y_far) + [win_spread], axis=2)
    got_y = lax.all_to_all(send_y, ("hx", "lo"), 1, 1, tiled=True)
    got_f = got_y[:, :, :4 * col_group].astype(jnp.float32)
    y_near_sum = jnp.sum(got_f[:, :, :col_group] + got_f[:, :, col_group:2 * col_group], axis=1)
    y_far_sum = jnp.sum(got_f[:, :, 2 * col_group:3 * col_group] + got_f[:, :, 3 * col_group:], axis=1)
    win_lo = lax.dynamic_slice_in_dim(got_y[:, :, 4 * col_group:], lax.axis_index("hx") * group, group, 1)
    wins = lax.all_gather(win_lo.reshape(tokens, group * ROW_DEV), "tok", axis=0, tiled=True)

    mirror = [(h * tok_count + t, (t ^ 1) * tok_count + h) for h in range(hi_count) for t in range(tok_count)]
    x_own = lax.ppermute(x_local, HI + ("tok",), swap)
    x_other = lax.ppermute(x_local, HI + ("tok",), mirror)
    swap_far = [(h * tok_count + t, t * tok_count + (h ^ 1)) for h in range(hi_count) for t in range(tok_count)]
    mirror_far = [(h * tok_count + t, (t ^ 1) * tok_count + (h ^ 1)) for h in range(hi_count) for t in range(tok_count)]
    near_pay = jnp.concatenate(halves(y_near_sum), axis=1)
    far_pay = jnp.concatenate(halves(y_far_sum), axis=1)

    def whole_y(near, far):
        parts = [near[:, :col_group], near[:, col_group:], far[:, :col_group], far[:, col_group:]]
        return jnp.concatenate(halves(sum(p.astype(jnp.float32) for p in parts)), axis=1)

    y_own = whole_y(lax.ppermute(near_pay, HI + ("tok",), swap), lax.ppermute(far_pay, HI + ("tok",), swap_far))
    y_other = whole_y(lax.ppermute(near_pay, HI + ("tok",), mirror), lax.ppermute(far_pay, HI + ("tok",), mirror_far))
    own = jnp.concatenate([x_own, y_own], axis=1)
    other = jnp.concatenate([x_other, y_other], axis=1)
    even_first = hy_index == 0
    pair = jnp.stack([jnp.where(even_first, own, other), jnp.where(even_first, other, own)])
    spread = jnp.broadcast_to(pair[None], (half_count,) + pair.shape)
    full = lax.all_to_all(spread, "hx", 0, 0, tiled=True)
    x_full = full[..., :span_width]
    y_tok = full[..., span_width:span_width + col_group].astype(jnp.float32) + full[..., span_width + col_group:].astype(jnp.float32)

    wins_split = wins.reshape(full.shape[:3] + (wins.shape[1],))
    over_tokens = (((0, 1, 2), (0, 1, 2)), ((), ()))
    gram = lax.dot_general(wins_split, x_full, over_tokens, preferred_element_type=jnp.float32)
    cross = lax.dot_general(
        wins_split.astype(jnp.float32), y_tok, over_tokens,
        precision=lax.Precision.HIGHEST, preferred_element_type=jnp.float32,
    )
    pieces = jnp.concatenate([gram, OFF_SCALE * cross], axis=1)
    pieces = pieces.reshape(group, ROW_DEV, span_width + col_group)

    win_own = lax.dynamic_slice_in_dim(wins, lo_index * ROW_DEV, ROW_DEV, 1).astype(jnp.float32)
    diag = jnp.sum(win_own * win_own, axis=0)
    w_cols = lax.dynamic_slice_in_dim(w_local, tok_index * tok_cols, tok_cols, 0)
    diag_term = (1.0 - OFF_SCALE) * diag[:, None] * w_cols[:, :ROW_DEV].astype(jnp.float32).T
    is_self = (jnp.arange(group) == lo_index)[:, None, None]
    diag_part = jnp.where(is_self, diag_term[None], 0.0)

    send = jnp.concatenate([pieces, diag_part], axis=2)
    send = jnp.concatenate([send] * mp_count, axis=0)
    got = lax.all_to_all(send, ("mp", "lo"), 0, 0, tiled=True)
    got = jnp.sum(got.reshape(mp_count, group, ROW_DEV, -1), axis=0)

    gram = got[:, :, :span_width]
    slot = lax.broadcasted_iota(jnp.int32, gram.shape, 0)
    row_ids = lax.broadcasted_iota(jnp.int32, gram.shape, 1)
    col_ids = lax.broadcasted_iota(jnp.int32, gram.shape, 2)
    on_diag = (tok_index == hi_index) & (slot == lo_index) & (col_ids == row_ids)
    reduced = jnp.where(on_diag, gram, OFF_SCALE * gram)
    denominator = jnp.transpose(reduced, (1, 0, 2)).reshape(ROW_DEV, group * span_width)
    numerator = jnp.transpose(got[:, :, span_width:span_width + col_group], (1, 0, 2)).reshape(ROW_DEV, tok_cols)
    numerator = numerator + jnp.sum(got[:, :, span_width + col_group:], axis=0)
    return (denominator, numerator)


def solution(mesh):
    mp_count, blk_count, tok_count = (mesh.shape[a] for a in ("mp", "blk", "tok"))
    group = blk_count // tok_count
    devices = np.asarray(mesh.devices).reshape(mp_count, tok_count // 2, 2, group, tok_count)
    split = Mesh(devices, ("mp",) + HI + ("lo", "tok"))
    placed = (P("mp", "tok", HI + ("lo",)), P("mp", None, HI + ("lo",)))
    return jax.shard_map(
        local,
        mesh=split,
        in_specs=placed,
        out_specs=(P(HI + ("lo",), "tok"), P(HI + ("lo",), "tok")),
        check_vma=False,
    )
```

```python
import jax
import jax.numpy as jnp
import numpy as np
from jax import lax
from jax.sharding import Mesh, PartitionSpec as P

ROW_DEV = 32
HI = ("hx", "hy")


OFF_SCALE = 0.9


def local(inputs, down_weight):
    x_local = inputs[0]
    w_local = down_weight[0]
    tokens, span_width = x_local.shape
    cols = w_local.shape[0]
    hi_index = lax.axis_index(HI)
    lo_index = lax.axis_index("lo")
    tok_index = lax.axis_index("tok")
    group = lax.axis_size("lo")
    hi_count = lax.axis_size(HI)
    half_count = lax.axis_size("hx")
    hy_index = lax.axis_index("hy")
    tok_count = lax.axis_size("tok")
    mp_count = lax.axis_size("mp")
    blk_count = hi_count * group
    col_group = cols // blk_count
    tok_cols = cols // tok_count

    swap = [(h * tok_count + t, t * tok_count + h) for h in range(hi_count) for t in range(tok_count)]

    y_part = lax.dot_general(
        x_local, w_local, (((1,), (1,)), ((), ())), preferred_element_type=jnp.float32
    )
    y_part_round = lax.reduce_precision(y_part, exponent_bits=8, mantissa_bits=7)
    y_part_high = y_part_round.astype(jnp.bfloat16).reshape(tokens, blk_count, col_group)
    y_part_low = (y_part - y_part_round).astype(jnp.bfloat16).reshape(tokens, blk_count, col_group)
    win_spread = jnp.broadcast_to(x_local[:, None, :ROW_DEV], (tokens, blk_count, ROW_DEV))
    send_y = jnp.concatenate([y_part_high, y_part_low, win_spread], axis=2)
    got_y = lax.all_to_all(send_y, HI + ("lo",), 1, 1, tiled=True)
    y_mine = jnp.sum(
        got_y[:, :, :col_group].astype(jnp.float32) + got_y[:, :, col_group:2 * col_group].astype(jnp.float32),
        axis=1,
    )
    win_lo = lax.dynamic_slice_in_dim(got_y[:, :, 2 * col_group:], hi_index * group, group, 1)
    wins = lax.all_gather(win_lo.reshape(tokens, group * ROW_DEV), "tok", axis=0, tiled=True)
    y_round = lax.reduce_precision(y_mine, exponent_bits=8, mantissa_bits=7)
    y_high = y_round.astype(jnp.bfloat16)
    y_low = (y_mine - y_round).astype(jnp.bfloat16)
    mirror = [(h * tok_count + t, (t ^ 1) * tok_count + h) for h in range(hi_count) for t in range(tok_count)]
    x_own = lax.ppermute(x_local, HI + ("tok",), swap)
    x_other = lax.ppermute(x_local, HI + ("tok",), mirror)
    y_pay = jnp.concatenate([y_high, y_low], axis=1)
    own = jnp.concatenate([x_own, lax.ppermute(y_pay, HI + ("tok",), swap)], axis=1)
    other = jnp.concatenate([x_other, lax.ppermute(y_pay, HI + ("tok",), mirror)], axis=1)
    even_first = hy_index == 0
    pair = jnp.stack([jnp.where(even_first, own, other), jnp.where(even_first, other, own)])
    spread = jnp.broadcast_to(pair[None], (half_count,) + pair.shape)
    full = lax.all_to_all(spread, "hx", 0, 0, tiled=True)
    x_full = full[..., :span_width]
    y_tok = full[..., span_width:span_width + col_group].astype(jnp.float32) + full[..., span_width + col_group:].astype(jnp.float32)

    wins_split = wins.reshape(full.shape[:3] + (wins.shape[1],))
    over_tokens = (((0, 1, 2), (0, 1, 2)), ((), ()))
    gram = lax.dot_general(wins_split, x_full, over_tokens, preferred_element_type=jnp.float32)
    cross = lax.dot_general(
        wins_split.astype(jnp.float32), y_tok, over_tokens,
        precision=lax.Precision.HIGHEST, preferred_element_type=jnp.float32,
    )
    pieces = jnp.concatenate([gram, OFF_SCALE * cross], axis=1)
    pieces = pieces.reshape(group, ROW_DEV, span_width + col_group)

    win_own = lax.dynamic_slice_in_dim(wins, lo_index * ROW_DEV, ROW_DEV, 1).astype(jnp.float32)
    diag = jnp.sum(win_own * win_own, axis=0)
    w_cols = lax.dynamic_slice_in_dim(w_local, tok_index * tok_cols, tok_cols, 0)
    diag_term = (1.0 - OFF_SCALE) * diag[:, None] * w_cols[:, :ROW_DEV].astype(jnp.float32).T
    is_self = (jnp.arange(group) == lo_index)[:, None, None]
    diag_part = jnp.where(is_self, diag_term[None], 0.0)

    send = jnp.concatenate([pieces, diag_part], axis=2)
    send = send + lax.ppermute(send, "mp", [(m, (m + 1) % mp_count) for m in range(mp_count)])
    got = lax.all_to_all(send, "lo", 0, 0, tiled=True)

    gram = got[:, :, :span_width]
    slot = lax.broadcasted_iota(jnp.int32, gram.shape, 0)
    row_ids = lax.broadcasted_iota(jnp.int32, gram.shape, 1)
    col_ids = lax.broadcasted_iota(jnp.int32, gram.shape, 2)
    on_diag = (tok_index == hi_index) & (slot == lo_index) & (col_ids == row_ids)
    reduced = jnp.where(on_diag, gram, OFF_SCALE * gram)
    denominator = jnp.transpose(reduced, (1, 0, 2)).reshape(ROW_DEV, group * span_width)
    numerator = jnp.transpose(got[:, :, span_width:span_width + col_group], (1, 0, 2)).reshape(ROW_DEV, tok_cols)
    numerator = numerator + jnp.sum(got[:, :, span_width + col_group:], axis=0)
    return (denominator, numerator)


def solution(mesh):
    mp_count, blk_count, tok_count = (mesh.shape[a] for a in ("mp", "blk", "tok"))
    group = blk_count // tok_count
    devices = np.asarray(mesh.devices).reshape(mp_count, tok_count // 2, 2, group, tok_count)
    split = Mesh(devices, ("mp",) + HI + ("lo", "tok"))
    placed = (P("mp", "tok", HI + ("lo",)), P("mp", None, HI + ("lo",)))
    return jax.shard_map(
        local,
        mesh=split,
        in_specs=placed,
        out_specs=(P(HI + ("lo",), "tok"), P(HI + ("lo",), "tok")),
        check_vma=False,
    )
```

```python
import jax
import jax.numpy as jnp
import numpy as np
from jax import lax
from jax.sharding import Mesh, PartitionSpec as P

ROW_DEV = 32
HI = ("hx", "hy")
TOK = ("tz", "tc")


OFF_SCALE = 0.9


def local(inputs, down_weight):
    x_local = inputs[0]
    w_local = down_weight[0]
    tokens, span_width = x_local.shape
    cols = w_local.shape[0]
    hi_index = lax.axis_index(HI)
    lo_index = lax.axis_index("lo")
    tok_index = lax.axis_index(TOK)
    group = lax.axis_size("lo")
    hi_count = lax.axis_size(HI)
    half_count = lax.axis_size("hx")
    hy_index = lax.axis_index("hy")
    tok_count = lax.axis_size(TOK)
    mp_count = lax.axis_size("mp")
    blk_count = hi_count * group
    col_group = cols // blk_count
    tok_cols = cols // tok_count

    swap = [(h * tok_count + t, t * tok_count + h) for h in range(hi_count) for t in range(tok_count)]

    y_part = lax.dot_general(
        x_local, w_local, (((1,), (1,)), ((), ())), preferred_element_type=jnp.float32
    )
    y_part_round = lax.reduce_precision(y_part, exponent_bits=8, mantissa_bits=7)
    y_part_high = y_part_round.astype(jnp.bfloat16).reshape(tokens, blk_count, col_group)
    y_part_low = (y_part - y_part_round).astype(jnp.bfloat16).reshape(tokens, blk_count, col_group)
    win_spread = jnp.broadcast_to(x_local[:, None, :ROW_DEV], (tokens, blk_count, ROW_DEV))
    send_y = jnp.concatenate([y_part_high, y_part_low, win_spread], axis=2)
    got_y = lax.all_to_all(send_y, HI + ("lo",), 1, 1, tiled=True)
    y_mine = jnp.sum(
        got_y[:, :, :col_group].astype(jnp.float32) + got_y[:, :, col_group:2 * col_group].astype(jnp.float32),
        axis=1,
    )
    win_lo = lax.dynamic_slice_in_dim(got_y[:, :, 2 * col_group:], hi_index * group, group, 1)
    wins = lax.all_gather(win_lo.reshape(tokens, group * ROW_DEV), "tc", axis=0, tiled=True)
    wins = lax.all_gather(wins, "tz", axis=0, tiled=True)
    y_round = lax.reduce_precision(y_mine, exponent_bits=8, mantissa_bits=7)
    y_high = y_round.astype(jnp.bfloat16)
    y_low = (y_mine - y_round).astype(jnp.bfloat16)
    mirror = [(h * tok_count + t, (t ^ 1) * tok_count + h) for h in range(hi_count) for t in range(tok_count)]
    x_own = lax.ppermute(x_local, HI + TOK, swap)
    x_other = lax.ppermute(x_local, HI + TOK, mirror)
    y_pay = jnp.concatenate([y_high, y_low], axis=1)
    own = jnp.concatenate([x_own, lax.ppermute(y_pay, HI + TOK, swap)], axis=1)
    other = jnp.concatenate([x_other, lax.ppermute(y_pay, HI + TOK, mirror)], axis=1)
    even_first = hy_index == 0
    pair = jnp.stack([jnp.where(even_first, own, other), jnp.where(even_first, other, own)])
    spread = jnp.broadcast_to(pair[None], (half_count,) + pair.shape)
    full = lax.all_to_all(spread, "hx", 0, 0, tiled=True)
    x_full = full[..., :span_width]
    y_tok = full[..., span_width:span_width + col_group].astype(jnp.float32) + full[..., span_width + col_group:].astype(jnp.float32)

    wins_split = wins.reshape(full.shape[:3] + (wins.shape[1],))
    over_tokens = (((0, 1, 2), (0, 1, 2)), ((), ()))
    gram = lax.dot_general(wins_split, x_full, over_tokens, preferred_element_type=jnp.float32)
    cross = lax.dot_general(
        wins_split.astype(jnp.float32), y_tok, over_tokens,
        precision=lax.Precision.HIGHEST, preferred_element_type=jnp.float32,
    )
    pieces = jnp.concatenate([gram, OFF_SCALE * cross], axis=1)
    pieces = pieces.reshape(group, ROW_DEV, span_width + col_group)

    win_own = lax.dynamic_slice_in_dim(wins, lo_index * ROW_DEV, ROW_DEV, 1).astype(jnp.float32)
    diag = jnp.sum(win_own * win_own, axis=0)
    w_cols = lax.dynamic_slice_in_dim(w_local, tok_index * tok_cols, tok_cols, 0)
    diag_term = (1.0 - OFF_SCALE) * diag[:, None] * w_cols[:, :ROW_DEV].astype(jnp.float32).T
    is_self = (jnp.arange(group) == lo_index)[:, None, None]
    diag_part = jnp.where(is_self, diag_term[None], 0.0)

    send = jnp.concatenate([pieces, diag_part], axis=2)
    send = jnp.concatenate([send] * mp_count, axis=0)
    got = lax.all_to_all(send, ("mp", "lo"), 0, 0, tiled=True)
    got = jnp.sum(got.reshape(mp_count, group, ROW_DEV, -1), axis=0)

    gram = got[:, :, :span_width]
    slot = lax.broadcasted_iota(jnp.int32, gram.shape, 0)
    row_ids = lax.broadcasted_iota(jnp.int32, gram.shape, 1)
    col_ids = lax.broadcasted_iota(jnp.int32, gram.shape, 2)
    on_diag = (tok_index == hi_index) & (slot == lo_index) & (col_ids == row_ids)
    reduced = jnp.where(on_diag, gram, OFF_SCALE * gram)
    denominator = jnp.transpose(reduced, (1, 0, 2)).reshape(ROW_DEV, group * span_width)
    numerator = jnp.transpose(got[:, :, span_width:span_width + col_group], (1, 0, 2)).reshape(ROW_DEV, tok_cols)
    numerator = numerator + jnp.sum(got[:, :, span_width + col_group:], axis=0)
    return (denominator, numerator)


def solution(mesh):
    mp_count, blk_count, tok_count = (mesh.shape[a] for a in ("mp", "blk", "tok"))
    group = blk_count // tok_count
    devices = np.asarray(mesh.devices).reshape(mp_count, tok_count // 2, 2, group, tok_count // 2, 2)
    split = Mesh(devices, ("mp",) + HI + ("lo",) + TOK)
    placed = (P("mp", TOK, HI + ("lo",)), P("mp", None, HI + ("lo",)))
    return jax.shard_map(
        local,
        mesh=split,
        in_specs=placed,
        out_specs=(P(HI + ("lo",), TOK), P(HI + ("lo",), TOK)),
        check_vma=False,
    )
```

```python
import jax
import jax.numpy as jnp
import numpy as np
from jax import lax
from jax.sharding import Mesh, PartitionSpec as P

ROW_DEV = 32
HI = ("hx", "hy")
TOK = ("tz", "tc")


OFF_SCALE = 0.9


def local(inputs, down_weight):
    x_local = inputs[0]
    w_local = down_weight[0]
    tokens, span_width = x_local.shape
    cols = w_local.shape[0]
    hi_index = lax.axis_index(HI)
    lo_index = lax.axis_index("lo")
    tok_index = lax.axis_index(TOK)
    group = lax.axis_size("lo")
    hi_count = lax.axis_size(HI)
    half_count = lax.axis_size("hx")
    hy_index = lax.axis_index("hy")
    tok_count = lax.axis_size(TOK)
    mp_count = lax.axis_size("mp")
    blk_count = hi_count * group
    col_group = cols // blk_count
    tok_cols = cols // tok_count

    swap = [(h * tok_count + t, t * tok_count + h) for h in range(hi_count) for t in range(tok_count)]

    y_part = lax.dot_general(
        x_local, w_local, (((1,), (1,)), ((), ())), preferred_element_type=jnp.float32
    )
    y_part_round = lax.reduce_precision(y_part, exponent_bits=8, mantissa_bits=7)
    y_part_high = y_part_round.astype(jnp.bfloat16).reshape(tokens, blk_count, col_group)
    y_part_low = (y_part - y_part_round).astype(jnp.bfloat16).reshape(tokens, blk_count, col_group)
    win_spread = jnp.broadcast_to(x_local[:, None, :ROW_DEV], (tokens, blk_count, ROW_DEV))
    send_y = jnp.concatenate([y_part_high, y_part_low, win_spread], axis=2)
    got_y = lax.all_to_all(send_y, HI + ("lo",), 1, 1, tiled=True)
    y_mine = jnp.sum(
        got_y[:, :, :col_group].astype(jnp.float32) + got_y[:, :, col_group:2 * col_group].astype(jnp.float32),
        axis=1,
    )
    win_lo = lax.dynamic_slice_in_dim(got_y[:, :, 2 * col_group:], hi_index * group, group, 1)
    wins = lax.all_gather(win_lo.reshape(tokens, group * ROW_DEV), "tc", axis=0, tiled=True)
    wins = lax.all_gather(wins, "tz", axis=0, tiled=True)
    y_round = lax.reduce_precision(y_mine, exponent_bits=8, mantissa_bits=7)
    y_high = y_round.astype(jnp.bfloat16)
    y_low = (y_mine - y_round).astype(jnp.bfloat16)
    mirror = [(h * tok_count + t, (t ^ 1) * tok_count + h) for h in range(hi_count) for t in range(tok_count)]
    x_own = lax.ppermute(x_local, HI + TOK, swap)
    x_other = lax.ppermute(x_local, HI + TOK, mirror)
    y_pay = jnp.concatenate([y_high, y_low], axis=1)
    own = jnp.concatenate([x_own, lax.ppermute(y_pay, HI + TOK, swap)], axis=1)
    other = jnp.concatenate([x_other, lax.ppermute(y_pay, HI + TOK, mirror)], axis=1)
    even_first = hy_index == 0
    pair = jnp.stack([own, other])
    spread = jnp.broadcast_to(pair[None], (half_count,) + pair.shape)
    full = lax.all_to_all(spread, "hx", 0, 0, tiled=True)
    x_full = full[..., :span_width]
    y_tok = full[..., span_width:span_width + col_group].astype(jnp.float32) + full[..., span_width + col_group:].astype(jnp.float32)

    wins_split = wins.reshape(full.shape[:3] + (wins.shape[1],))
    wins_split = jnp.where(even_first, wins_split, wins_split[:, ::-1])
    over_tokens = (((0, 1, 2), (0, 1, 2)), ((), ()))
    gram = lax.dot_general(wins_split, x_full, over_tokens, preferred_element_type=jnp.float32)
    cross = lax.dot_general(
        wins_split.astype(jnp.float32), y_tok, over_tokens,
        precision=lax.Precision.HIGHEST, preferred_element_type=jnp.float32,
    )
    pieces = jnp.concatenate([gram, OFF_SCALE * cross], axis=1)
    pieces = pieces.reshape(group, ROW_DEV, span_width + col_group)

    win_own = lax.dynamic_slice_in_dim(wins, lo_index * ROW_DEV, ROW_DEV, 1).astype(jnp.float32)
    diag = jnp.sum(win_own * win_own, axis=0)
    w_cols = lax.dynamic_slice_in_dim(w_local, tok_index * tok_cols, tok_cols, 0)
    diag_term = (1.0 - OFF_SCALE) * diag[:, None] * w_cols[:, :ROW_DEV].astype(jnp.float32).T
    is_self = (jnp.arange(group) == lo_index)[:, None, None]
    diag_part = jnp.where(is_self, diag_term[None], 0.0)

    send = jnp.concatenate([pieces, diag_part], axis=2)
    send = jnp.concatenate([send] * mp_count, axis=0)
    got = lax.all_to_all(send, ("mp", "lo"), 0, 0, tiled=True)
    got = jnp.sum(got.reshape(mp_count, group, ROW_DEV, -1), axis=0)

    gram = got[:, :, :span_width]
    slot = lax.broadcasted_iota(jnp.int32, gram.shape, 0)
    row_ids = lax.broadcasted_iota(jnp.int32, gram.shape, 1)
    col_ids = lax.broadcasted_iota(jnp.int32, gram.shape, 2)
    on_diag = (tok_index == hi_index) & (slot == lo_index) & (col_ids == row_ids)
    reduced = jnp.where(on_diag, gram, OFF_SCALE * gram)
    denominator = jnp.transpose(reduced, (1, 0, 2)).reshape(ROW_DEV, group * span_width)
    numerator = jnp.transpose(got[:, :, span_width:span_width + col_group], (1, 0, 2)).reshape(ROW_DEV, tok_cols)
    numerator = numerator + jnp.sum(got[:, :, span_width + col_group:], axis=0)
    return (denominator, numerator)


def solution(mesh):
    mp_count, blk_count, tok_count = (mesh.shape[a] for a in ("mp", "blk", "tok"))
    group = blk_count // tok_count
    devices = np.asarray(mesh.devices).reshape(mp_count, tok_count // 2, 2, group, tok_count // 2, 2)
    split = Mesh(devices, ("mp",) + HI + ("lo",) + TOK)
    placed = (P("mp", TOK, HI + ("lo",)), P("mp", None, HI + ("lo",)))
    return jax.shard_map(
        local,
        mesh=split,
        in_specs=placed,
        out_specs=(P(HI + ("lo",), TOK), P(HI + ("lo",), TOK)),
        check_vma=False,
    )
```

```python
import jax
import jax.numpy as jnp
import numpy as np
from jax import lax
from jax.sharding import Mesh, PartitionSpec as P

ROW_DEV = 32
HI = ("hx", "hy")
TOK = ("tz", "tc")


OFF_SCALE = 0.9


def local(inputs, down_weight):
    x_local = inputs[0]
    w_local = down_weight[0]
    tokens, span_width = x_local.shape
    cols = w_local.shape[0]
    hi_index = lax.axis_index(HI)
    lo_index = lax.axis_index("lo")
    tok_index = lax.axis_index(TOK)
    group = lax.axis_size("lo")
    hi_count = lax.axis_size(HI)
    half_count = lax.axis_size("hx")
    hy_index = lax.axis_index("hy")
    tok_count = lax.axis_size(TOK)
    mp_count = lax.axis_size("mp")
    blk_count = hi_count * group
    col_group = cols // blk_count
    tok_cols = cols // tok_count

    swap = [(h * tok_count + t, t * tok_count + h) for h in range(hi_count) for t in range(tok_count)]

    y_part = lax.dot_general(
        x_local, w_local, (((1,), (1,)), ((), ())), preferred_element_type=jnp.float32
    )
    y_part_round = lax.reduce_precision(y_part, exponent_bits=8, mantissa_bits=7)
    y_part_high = y_part_round.astype(jnp.bfloat16).reshape(tokens, blk_count, col_group)
    y_part_low = (y_part - y_part_round).astype(jnp.bfloat16).reshape(tokens, blk_count, col_group)
    win_spread = jnp.broadcast_to(x_local[:, None, :ROW_DEV], (tokens, blk_count, ROW_DEV))
    send_y = jnp.concatenate([y_part_high, y_part_low, win_spread], axis=2)
    got_y = lax.all_to_all(send_y, HI + ("lo",), 1, 1, tiled=True)
    y_mine = jnp.sum(
        got_y[:, :, :col_group].astype(jnp.float32) + got_y[:, :, col_group:2 * col_group].astype(jnp.float32),
        axis=1,
    )
    win_lo = lax.dynamic_slice_in_dim(got_y[:, :, 2 * col_group:], hi_index * group, group, 1)
    wins = lax.all_gather(win_lo.reshape(tokens, group * ROW_DEV), "tc", axis=0, tiled=True)
    wins = lax.all_gather(wins, "tz", axis=0, tiled=True)
    y_round = lax.reduce_precision(y_mine, exponent_bits=8, mantissa_bits=7)
    y_high = y_round.astype(jnp.bfloat16)
    y_low = (y_mine - y_round).astype(jnp.bfloat16)
    mirror = [(h * tok_count + t, (t ^ 1) * tok_count + h) for h in range(hi_count) for t in range(tok_count)]
    x_own = lax.ppermute(x_local, HI + TOK, swap)
    x_other = lax.ppermute(x_local, HI + TOK, mirror)
    y_pay = jnp.concatenate([y_high, y_low], axis=1)
    own = jnp.concatenate([x_own, lax.ppermute(y_pay, HI + TOK, swap)], axis=1)
    other = jnp.concatenate([x_other, lax.ppermute(y_pay, HI + TOK, mirror)], axis=1)
    even_first = hy_index == 0
    pair = jnp.stack([own, other])
    full = lax.all_gather(pair, "hx", axis=0, tiled=False)
    x_full = full[..., :span_width]
    y_tok = full[..., span_width:span_width + col_group].astype(jnp.float32) + full[..., span_width + col_group:].astype(jnp.float32)

    wins_split = wins.reshape(full.shape[:3] + (wins.shape[1],))
    wins_split = jnp.where(even_first, wins_split, wins_split[:, ::-1])
    over_tokens = (((0, 1, 2), (0, 1, 2)), ((), ()))
    gram = lax.dot_general(wins_split, x_full, over_tokens, preferred_element_type=jnp.float32)
    cross = lax.dot_general(
        wins_split.astype(jnp.float32), y_tok, over_tokens,
        precision=lax.Precision.HIGHEST, preferred_element_type=jnp.float32,
    )
    pieces = jnp.concatenate([gram, OFF_SCALE * cross], axis=1)
    pieces = pieces.reshape(group, ROW_DEV, span_width + col_group)

    win_own = lax.dynamic_slice_in_dim(wins, lo_index * ROW_DEV, ROW_DEV, 1).astype(jnp.float32)
    diag = jnp.sum(win_own * win_own, axis=0)
    w_cols = lax.dynamic_slice_in_dim(w_local, tok_index * tok_cols, tok_cols, 0)
    diag_term = (1.0 - OFF_SCALE) * diag[:, None] * w_cols[:, :ROW_DEV].astype(jnp.float32).T
    is_self = (jnp.arange(group) == lo_index)[:, None, None]
    diag_part = jnp.where(is_self, diag_term[None], 0.0)

    send = jnp.concatenate([pieces, diag_part], axis=2)
    send = jnp.concatenate([send] * mp_count, axis=0)
    got = lax.all_to_all(send, ("mp", "lo"), 0, 0, tiled=True)
    got = jnp.sum(got.reshape(mp_count, group, ROW_DEV, -1), axis=0)

    gram = got[:, :, :span_width]
    slot = lax.broadcasted_iota(jnp.int32, gram.shape, 0)
    row_ids = lax.broadcasted_iota(jnp.int32, gram.shape, 1)
    col_ids = lax.broadcasted_iota(jnp.int32, gram.shape, 2)
    on_diag = (tok_index == hi_index) & (slot == lo_index) & (col_ids == row_ids)
    reduced = jnp.where(on_diag, gram, OFF_SCALE * gram)
    denominator = jnp.transpose(reduced, (1, 0, 2)).reshape(ROW_DEV, group * span_width)
    numerator = jnp.transpose(got[:, :, span_width:span_width + col_group], (1, 0, 2)).reshape(ROW_DEV, tok_cols)
    numerator = numerator + jnp.sum(got[:, :, span_width + col_group:], axis=0)
    return (denominator, numerator)


def solution(mesh):
    mp_count, blk_count, tok_count = (mesh.shape[a] for a in ("mp", "blk", "tok"))
    group = blk_count // tok_count
    devices = np.asarray(mesh.devices).reshape(mp_count, tok_count // 2, 2, group, tok_count // 2, 2)
    split = Mesh(devices, ("mp",) + HI + ("lo",) + TOK)
    placed = (P("mp", TOK, HI + ("lo",)), P("mp", None, HI + ("lo",)))
    return jax.shard_map(
        local,
        mesh=split,
        in_specs=placed,
        out_specs=(P(HI + ("lo",), TOK), P(HI + ("lo",), TOK)),
        check_vma=False,
    )
```

```python
import jax
import jax.numpy as jnp
import numpy as np
from jax import lax
from jax.sharding import Mesh, PartitionSpec as P

ROW_DEV = 32
HI = ("hx", "hy")
TOK = ("tz", "tc")


OFF_SCALE = 0.9


def local(inputs, down_weight):
    x_local = inputs[0]
    w_local = down_weight[0]
    tokens, span_width = x_local.shape
    cols = w_local.shape[0]
    hi_index = lax.axis_index(HI)
    lo_index = lax.axis_index("lo")
    tok_index = lax.axis_index(TOK)
    group = lax.axis_size("lo")
    hi_count = lax.axis_size(HI)
    half_count = lax.axis_size("hx")
    hy_index = lax.axis_index("hy")
    tok_count = lax.axis_size(TOK)
    mp_count = lax.axis_size("mp")
    blk_count = hi_count * group
    col_group = cols // blk_count
    tok_cols = cols // tok_count

    swap = [(h * tok_count + t, t * tok_count + h) for h in range(hi_count) for t in range(tok_count)]

    y_part = lax.dot_general(
        x_local, w_local, (((1,), (1,)), ((), ())), preferred_element_type=jnp.float32
    )
    y_part_round = lax.reduce_precision(y_part, exponent_bits=8, mantissa_bits=7)
    y_part_high = y_part_round.astype(jnp.bfloat16).reshape(tokens, blk_count, col_group)
    y_part_low = (y_part - y_part_round).astype(jnp.bfloat16).reshape(tokens, blk_count, col_group)
    win_spread = jnp.broadcast_to(x_local[:, None, :ROW_DEV], (tokens, blk_count, ROW_DEV))
    send_y = jnp.concatenate([y_part_high, y_part_low, win_spread], axis=2)
    got_y = lax.all_to_all(send_y, HI + ("lo",), 1, 1, tiled=True)
    y_mine = jnp.sum(
        got_y[:, :, :col_group].astype(jnp.float32) + got_y[:, :, col_group:2 * col_group].astype(jnp.float32),
        axis=1,
    )
    win_lo = lax.dynamic_slice_in_dim(got_y[:, :, 2 * col_group:], hi_index * group, group, 1)
    wins = lax.all_gather(win_lo.reshape(tokens, group * ROW_DEV), "tz", axis=0, tiled=False)
    wins = lax.all_gather(wins, "tc", axis=1, tiled=False)
    wins = wins.reshape(tok_count * tokens, group * ROW_DEV)
    y_round = lax.reduce_precision(y_mine, exponent_bits=8, mantissa_bits=7)
    y_high = y_round.astype(jnp.bfloat16)
    y_low = (y_mine - y_round).astype(jnp.bfloat16)
    mirror = [(h * tok_count + t, (t ^ 1) * tok_count + h) for h in range(hi_count) for t in range(tok_count)]
    x_own = lax.ppermute(x_local, HI + TOK, swap)
    x_other = lax.ppermute(x_local, HI + TOK, mirror)
    y_pay = jnp.concatenate([y_high, y_low], axis=1)
    own = jnp.concatenate([x_own, lax.ppermute(y_pay, HI + TOK, swap)], axis=1)
    other = jnp.concatenate([x_other, lax.ppermute(y_pay, HI + TOK, mirror)], axis=1)
    even_first = hy_index == 0
    pair = jnp.stack([own, other])
    spread = jnp.broadcast_to(pair[None], (half_count,) + pair.shape)
    full = lax.all_to_all(spread, "hx", 0, 0, tiled=True)
    x_full = full[..., :span_width]
    y_tok = full[..., span_width:span_width + col_group].astype(jnp.float32) + full[..., span_width + col_group:].astype(jnp.float32)

    wins_split = wins.reshape(full.shape[:3] + (wins.shape[1],))
    wins_split = jnp.where(even_first, wins_split, wins_split[:, ::-1])
    over_tokens = (((0, 1, 2), (0, 1, 2)), ((), ()))
    gram = lax.dot_general(wins_split, x_full, over_tokens, preferred_element_type=jnp.float32)
    cross = lax.dot_general(
        wins_split.astype(jnp.float32), y_tok, over_tokens,
        precision=lax.Precision.HIGHEST, preferred_element_type=jnp.float32,
    )
    pieces = jnp.concatenate([gram, OFF_SCALE * cross], axis=1)
    pieces = pieces.reshape(group, ROW_DEV, span_width + col_group)

    win_own = lax.dynamic_slice_in_dim(wins, lo_index * ROW_DEV, ROW_DEV, 1).astype(jnp.float32)
    diag = jnp.sum(win_own * win_own, axis=0)
    w_cols = lax.dynamic_slice_in_dim(w_local, tok_index * tok_cols, tok_cols, 0)
    diag_term = (1.0 - OFF_SCALE) * diag[:, None] * w_cols[:, :ROW_DEV].astype(jnp.float32).T
    is_self = (jnp.arange(group) == lo_index)[:, None, None]
    diag_part = jnp.where(is_self, diag_term[None], 0.0)

    send = jnp.concatenate([pieces, diag_part], axis=2)
    send = jnp.concatenate([send] * mp_count, axis=0)
    got = lax.all_to_all(send, ("mp", "lo"), 0, 0, tiled=True)
    got = jnp.sum(got.reshape(mp_count, group, ROW_DEV, -1), axis=0)

    gram = got[:, :, :span_width]
    slot = lax.broadcasted_iota(jnp.int32, gram.shape, 0)
    row_ids = lax.broadcasted_iota(jnp.int32, gram.shape, 1)
    col_ids = lax.broadcasted_iota(jnp.int32, gram.shape, 2)
    on_diag = (tok_index == hi_index) & (slot == lo_index) & (col_ids == row_ids)
    reduced = jnp.where(on_diag, gram, OFF_SCALE * gram)
    denominator = jnp.transpose(reduced, (1, 0, 2)).reshape(ROW_DEV, group * span_width)
    numerator = jnp.transpose(got[:, :, span_width:span_width + col_group], (1, 0, 2)).reshape(ROW_DEV, tok_cols)
    numerator = numerator + jnp.sum(got[:, :, span_width + col_group:], axis=0)
    return (denominator, numerator)


def solution(mesh):
    mp_count, blk_count, tok_count = (mesh.shape[a] for a in ("mp", "blk", "tok"))
    group = blk_count // tok_count
    devices = np.asarray(mesh.devices).reshape(mp_count, tok_count // 2, 2, group, tok_count // 2, 2)
    split = Mesh(devices, ("mp",) + HI + ("lo",) + TOK)
    placed = (P("mp", TOK, HI + ("lo",)), P("mp", None, HI + ("lo",)))
    return jax.shard_map(
        local,
        mesh=split,
        in_specs=placed,
        out_specs=(P(HI + ("lo",), TOK), P(HI + ("lo",), TOK)),
        check_vma=False,
    )
```
